32 devices in a mesh: dp: 8 (over z, core), tensor: 4 (over y, x).
Axes of the slice: x: 2, y: 2, z: 4, core: 2. Of those that a mesh axis runs over, the one named last changes fastest.
Arguments:
- inputs: bfloat16 [8192, 2048], P(('dp', 'tensor')), may hold values from -6 to 6
- teacher: bfloat16 [8192, 2048], P(('dp', 'tensor')), may hold values from -6 to 6
- segment: int32 [8192], P('dp'), may hold values from 0 to 13, as said below
- position: int32 [8192], P('dp'), may hold values from 0 to 1023, as said below
- wq: bfloat16 [2048, 2048], P('dp', 'tensor'), may hold values from -0.125 to 0.125
- wk: bfloat16 [2048, 2048], P('dp', 'tensor'), may hold values from -0.125 to 0.125
- wv: bfloat16 [2048, 2048], P('dp', 'tensor'), may hold values from -0.125 to 0.125
- wo: bfloat16 [2048, 2048], P('tensor', 'dp'), may hold values from -0.125 to 0.125
- wg: bfloat16 [2048, 8192], P('dp', 'tensor'), may hold values from -0.125 to 0.125
- wu: bfloat16 [2048, 8192], P('dp', 'tensor'), may hold values from -0.125 to 0.125
- wd: bfloat16 [8192, 2048], P('tensor', 'dp'), may hold values from -0.0625 to 0.0625
- q_gain: bfloat16 [2048], P('dp'), may hold values from 0.099609375 to 1.8984375
- k_gain: bfloat16 [2048], P('dp'), may hold values from 0.099609375 to 1.8984375
- attn_gain: bfloat16 [2048], P('dp'), may hold values from 0.099609375 to 1.8984375
- ffn_gain: bfloat16 [2048], P('dp'), may hold values from 0.099609375 to 1.8984375
Outputs:
- output: bfloat16 [8192, 2048], P(('dp', 'tensor'))
- loss: float32 [], replicated
- grad_x: float32 [8192, 2048], P(('dp', 'tensor'))
- grad_wq: float32 [2048, 2048], P('dp', 'tensor')
- grad_wk: float32 [2048, 2048], P('dp', 'tensor')
- grad_wv: float32 [2048, 2048], P('dp', 'tensor')
- grad_wo: float32 [2048, 2048], P('tensor', 'dp')
- grad_wg: float32 [2048, 8192], P('dp', 'tensor')
- grad_wu: float32 [2048, 8192], P('dp', 'tensor')
- grad_wd: float32 [8192, 2048], P('tensor', 'dp')
- grad_q_gain: float32 [2048], P('dp')
- grad_k_gain: float32 [2048], P('dp')
- grad_attn_gain: float32 [2048], P('dp')
- grad_ffn_gain: float32 [2048], P('dp')
The draws below stay inside these ranges and needn't reach their ends.
Inputs may be any that keep to these rules, and one draw needn't show every extreme that they name: `segment`: each sequence is 1024 consecutive tokens; in it, documents are runs of one nonzero number that never falls, followed at the sequence's end by a run of zeros (padding), which may be empty. Numbers repeat in other sequences. Sequence 0 is one whole document; sequence 1 holds thirteen. `position`: each token's index within its document; padding tokens count from the start of their padding run.
All inputs are finite; a program needn't handle non-finite values.
Results may differ from the reference program's by a relative error of at most 0.025.
Values may be sent and summed in bfloat16 or wider, within the bound.
No kernel may reach another device: no remote copies, remote signals or barrier semaphores. Data moves between devices by JAX's collectives and lax.ppermute only.
A program may use at most 192 MiB of HBM per device.

```python
import jax
import jax.numpy as jnp
from jax import lax

D = 2048
HEADS = 16
HD = 128
FF = 8192
LEN = 1024
SEQS = 8
TOKENS = 8192


def packing(key):
    first_key, second_key, used_key, pad_key = jax.random.split(jax.random.fold_in(key, 11), 4)
    first = jax.random.randint(first_key, (SEQS, 12), 1, LEN)
    second = jax.random.randint(second_key, (SEQS, 12), 1, LEN)
    cuts = jnp.maximum(first * second // LEN, 1)
    used = jax.random.randint(used_key, (SEQS, 1), 2, 13)
    slots = jnp.arange(12)[None, :]
    cuts = jnp.where(slots < used, cuts, LEN)
    seq_index = jnp.arange(SEQS)[:, None]
    cuts = jnp.where(seq_index == 0, LEN, cuts)
    cuts = jnp.where(seq_index == 1, slots + 1, cuts)
    padding = seq_index * LEN * 2 // (3 * SEQS) + jax.random.randint(pad_key, (SEQS, 1), 0, LEN // 8 + 1)
    padding = jnp.where(seq_index == 0, 0, padding)
    limit = LEN - padding
    places = jnp.arange(LEN)[None, :, None]
    passed = places >= cuts[:, None, :]
    numbers = 1 + jnp.sum(passed.astype(jnp.int32), axis=-1)
    starts = jnp.max(jnp.where(passed, cuts[:, None, :], 0), axis=-1)
    in_padding = jnp.arange(LEN)[None, :] >= limit
    numbers = jnp.where(in_padding, 0, numbers)
    starts = jnp.where(in_padding, limit, starts)
    offsets = jnp.arange(LEN)[None, :] - starts
    return (numbers.reshape(-1).astype(jnp.int32), offsets.reshape(-1).astype(jnp.int32))


def draw_segment(key, part):
    return packing(key)[0]


def draw_position(key, part):
    return packing(key)[1]


def steps_of(own_key, shape, shards, smallest, largest):
    level = 1.0
    for axis_at, shards_of in shards:
        draws = jax.random.uniform(jax.random.fold_in(jax.random.fold_in(own_key, 6), axis_at), (shards_of,), jnp.float32, smallest / len(shards), largest / len(shards))
        level = level * jnp.repeat(jnp.exp(draws), shape[axis_at] // shards_of).reshape((-1,) + (1,) * (len(shape) - 1 - axis_at))
    return level


def centred(rng, dims, width, reach, cuts=(), held_as=jnp.bfloat16):
    level = steps_of(rng, dims, cuts, -0.22, 0.18) if cuts else 1.0
    result = jax.random.normal(rng, dims, jnp.float32) * width * level
    return jnp.minimum(jnp.maximum(result, -reach), reach).astype(held_as)


def setup_inputs(seed: int = 0) -> dict:
    key_of = jax.random.split(jax.random.key(seed), 16)
    return {
        "inputs": centred(key_of[0], (TOKENS, D), 1.0, 6.0, ((0, 32),)),
        "teacher": centred(key_of[1], (TOKENS, D), 1.0, 6.0, ((0, 32),)),
        "segment": draw_segment(jax.random.fold_in(key_of[15], 71), 0),
        "position": draw_position(jax.random.fold_in(key_of[15], 71), 0),
        "wq": centred(key_of[4], (D, D), D ** -0.5, 0.125, ((0, 8), (1, 4))),
        "wk": centred(key_of[5], (D, D), D ** -0.5, 0.125, ((0, 8), (1, 4))),
        "wv": centred(key_of[6], (D, D), D ** -0.5, 0.125, ((0, 8), (1, 4))),
        "wo": centred(key_of[7], (D, D), D ** -0.5, 0.125, ((0, 4), (1, 8))),
        "wg": centred(key_of[8], (D, FF), D ** -0.5, 0.125, ((0, 8), (1, 4))),
        "wu": centred(key_of[9], (D, FF), D ** -0.5, 0.125, ((0, 8), (1, 4))),
        "wd": centred(key_of[10], (FF, D), FF ** -0.5, 0.0625, ((0, 4), (1, 8))),
        "q_gain": jnp.clip(1.0 + 0.18 * jax.random.normal(key_of[11], (D,), jnp.float32), 0.099609375, 1.8984375).astype(jnp.bfloat16),
        "k_gain": jnp.clip(1.0 + 0.18 * jax.random.normal(key_of[12], (D,), jnp.float32), 0.099609375, 1.8984375).astype(jnp.bfloat16),
        "attn_gain": jnp.clip(1.0 + 0.18 * jax.random.normal(key_of[13], (D,), jnp.float32), 0.099609375, 1.8984375).astype(jnp.bfloat16),
        "ffn_gain": jnp.clip(1.0 + 0.18 * jax.random.normal(key_of[14], (D,), jnp.float32), 0.099609375, 1.8984375).astype(jnp.bfloat16),
    }


@jax.custom_vjp
def low(v):
    return lax.optimization_barrier(v.astype(jnp.bfloat16)).astype(jnp.float32)

@jax.custom_vjp
def low_back(v):
    return v

def low_keep(v):
    return (low(v), None)

def low_pass(kept, grad):
    return (grad,)

def back_keep(v):
    return (v, None)

def back_low(kept, grad):
    return (low(grad),)
low.defvjp(low_keep, low_pass)
low_back.defvjp(back_keep, back_low)
EPS = 1e-06
THETA = 500000.0
NEGATIVE = -1e+30
HIGHEST = lax.Precision.HIGHEST

def matmul(left, right):
    return jnp.dot(left, right, precision=HIGHEST, preferred_element_type=jnp.float32)

def rms_norm(values, gain):
    return values * lax.rsqrt(lax.optimization_barrier(jnp.mean(values * values, axis=-1, keepdims=True)) + EPS) * gain

def tables(position):
    freq = 1.0 / THETA ** (jnp.arange(0, HD, 2).astype(jnp.float32) / HD)
    angle = position.astype(jnp.float32)[:, None] * freq[None, :]
    angle = jnp.concatenate([angle, angle], axis=1)[:, None, :]
    return (jnp.cos(angle), jnp.sin(angle))

def rotate(values, cosines, sines):
    half = values.shape[-1] // 2
    turned = jnp.concatenate([-values[..., half:], values[..., :half]], axis=-1)
    return values * cosines + turned * sines

def allowed_keys(segment):
    length = segment.shape[0]
    place = lax.broadcasted_iota(jnp.int32, (length, length), 0)
    other = lax.broadcasted_iota(jnp.int32, (length, length), 1)
    return (segment[:, None] == segment[None, :]) & (place >= other)

def attend(pack):
    query, key, value, segment = pack
    scores = jnp.einsum('qhd,khd->hqk', query, key, precision=HIGHEST) * HD ** (-0.5)
    scores = jnp.where(allowed_keys(segment)[None], low_back(scores), NEGATIVE)
    highest = lax.optimization_barrier(jnp.max(scores, axis=-1, keepdims=True))
    raised = jnp.exp(scores - highest)
    prob = low(raised / lax.optimization_barrier(jnp.sum(raised, axis=-1, keepdims=True)))
    return jnp.einsum('hqk,khd->qhd', prob, value, precision=HIGHEST)

def layer(inputs, wq, wk, wv, wo, wg, wu, wd, q_gain, k_gain, attn_gain, ffn_gain, cosines, sines, segment):
    rows = inputs.shape[0]
    raw_q = low_back(matmul(inputs, wq))
    raw_k = low_back(matmul(inputs, wk))
    value = low(low_back(matmul(inputs, wv))).reshape(rows, HEADS, HD)
    query = low(rotate(rms_norm(raw_q, q_gain).reshape(rows, HEADS, HD), cosines, sines))
    key = low(rotate(rms_norm(raw_k, k_gain).reshape(rows, HEADS, HD), cosines, sines))
    sequences = rows // LEN
    blocks = (sequences, LEN, HEADS, HD)
    mixed = lax.map(jax.checkpoint(attend), (query.reshape(blocks), key.reshape(blocks), value.reshape(blocks), segment.reshape(sequences, LEN)))
    mixed = low(low_back(mixed.reshape(rows, D)))
    resid = inputs + rms_norm(low_back(matmul(mixed, wo)), attn_gain)
    resid_low = low(resid)
    gate = low_back(matmul(resid_low, wg))
    up = low_back(matmul(resid_low, wu))
    hidden = low(jax.nn.silu(gate) * up)
    return resid + rms_norm(low_back(matmul(hidden, wd)), ffn_gain)

def reference(inputs, teacher, segment, position, wq, wk, wv, wo, wg, wu, wd, q_gain, k_gain, attn_gain, ffn_gain):
    cosines, sines = tables(position)
    valid = (segment != 0).astype(jnp.float32)
    count = jnp.sum(valid)
    target = teacher.astype(jnp.float32)
    params = tuple((item.astype(jnp.float32) for item in (inputs, wq, wk, wv, wo, wg, wu, wd, q_gain, k_gain, attn_gain, ffn_gain)))

    def objective(*arrays):
        output = layer(*arrays, cosines, sines, segment)
        error = output - target
        loss = jnp.sum(valid[:, None] * error * error) / (count * D)
        return (loss * float(TOKENS * D), (output, loss))
    scaled, pull, extra = jax.vjp(objective, *params, has_aux=True)
    output, loss = extra
    grads = pull(jnp.ones((), jnp.float32))
    return (output.astype(jnp.bfloat16), loss, grads[0], grads[1], grads[2], grads[3], grads[4], grads[5], grads[6], grads[7], grads[8], grads[9], grads[10], grads[11])
```

```python
import jax
import jax.numpy as jnp
from jax import lax
from jax.sharding import PartitionSpec as P

HD = 128
LEN = 1024
EPS = 1e-06
THETA = 500000.0
NEGATIVE = -1e30
BF = jnp.bfloat16
F32 = jnp.float32


def tables(position):
    freq = 1.0 / THETA ** (jnp.arange(0, HD, 2).astype(F32) / HD)
    angle = position.astype(F32)[:, None] * freq[None, :]
    angle = jnp.concatenate([angle, angle], axis=1)[:, None, :]
    return (jnp.cos(angle), jnp.sin(angle))


def rotate(values, cosines, sines):
    half = values.shape[-1] // 2
    turned = jnp.concatenate([-values[..., half:], values[..., :half]], axis=-1)
    return values * cosines + turned * sines


def unrotate(grad, cosines, sines):
    half = grad.shape[-1] // 2
    turned = grad * sines
    return grad * cosines + jnp.concatenate([turned[..., half:], -turned[..., :half]], axis=-1)


def inner_rows(left, right):
    return lax.dot_general(left, right, (((0,), (0,)), ((), ())), preferred_element_type=F32)


def times(left, right):
    return jnp.dot(left, right, preferred_element_type=F32)


def times_transposed(left, right):
    return lax.dot_general(left, right, (((1,), (1,)), ((), ())), preferred_element_type=F32)


def hop(value, way, size=4):
    return lax.ppermute(value, "tensor", [(i, i ^ way) for i in range(size)])


class Square:
    def __init__(self, size):
        self.size = size
        self.me = lax.axis_index("tensor")
        self.order = self.me ^ jnp.arange(size)

    def gather(self, own):
        half = own.shape[0] // 2
        across = hop(own, 1)
        along = hop(own, 2)
        first = hop(across[:half], 2)
        second = hop(along[half:], 1)
        return jnp.concatenate([own, across, along, first, second], axis=0)

    def scatter(self, parts):
        rows = parts.shape[0] // 4
        half = rows // 2
        own, across, along, far = (parts[i * rows : (i + 1) * rows] for i in range(4))
        far = far.astype(BF)
        first = hop(far[:half], 1).astype(F32)
        second = hop(far[half:], 2).astype(F32)
        along = jnp.concatenate([along[:half] + first, along[half:]], axis=0).astype(BF)
        across = jnp.concatenate([across[:half], across[half:] + second], axis=0).astype(BF)
        return own + hop(across, 1).astype(F32) + hop(along, 2).astype(F32)

    def total(self, value):
        return (value + hop(value, 1)) + (hop(value, 2) + hop(value, 3))

    def total_by_token(self, value):
        blocks = value.reshape(value.shape[0], 4, -1)
        result = blocks
        for way in (1, 2, 3):
            got = hop(blocks, way)
            result = result + jnp.stack([got[:, r ^ way] for r in range(4)], axis=1)
        return result.reshape(value.shape)


class Plain:
    def __init__(self, size):
        self.size = size
        self.me = lax.axis_index("tensor")
        self.order = jnp.arange(size)

    def gather(self, own):
        return lax.all_gather(own, "tensor", axis=0, tiled=True)

    def scatter(self, parts):
        return lax.psum_scatter(
            parts.astype(BF), "tensor", scatter_dimension=0, tiled=True
        ).astype(F32)

    def total(self, value):
        return lax.psum(value, "tensor")

    def total_by_token(self, value):
        return lax.psum(value, "tensor")


def attend_forward(query, key, value, allowed):
    scores = jnp.einsum("qhd,khd->hqk", query, key, preferred_element_type=F32) * HD ** (-0.5)
    scores = jnp.where(allowed[None], scores, NEGATIVE)
    highest = jnp.max(scores, axis=-1, keepdims=True)
    raised = jnp.exp(scores - highest)
    total = jnp.sum(raised, axis=-1, keepdims=True)
    prob = (raised / total).astype(BF)
    mixed = jnp.einsum("hqk,khd->qhd", prob, value, preferred_element_type=F32)
    return (mixed.astype(BF), (highest + jnp.log(total))[..., 0])


def attend_backward(query, key, value, allowed, logsum, grad_mixed):
    scores = jnp.einsum("qhd,khd->hqk", query, key, preferred_element_type=F32) * HD ** (-0.5)
    scores = jnp.where(allowed[None], scores, NEGATIVE)
    prob = jnp.exp(scores - logsum[..., None])
    grad_prob = jnp.einsum("qhd,khd->hqk", grad_mixed, value, preferred_element_type=F32)
    delta = jnp.sum(grad_prob * prob, axis=-1, keepdims=True)
    grad_scores = (prob * (grad_prob - delta)).astype(BF)
    factor = HD ** (-0.5)
    grad_value = jnp.einsum("hqk,qhd->khd", prob.astype(BF), grad_mixed, preferred_element_type=F32)
    grad_query = jnp.einsum("hqk,khd->qhd", grad_scores, key, preferred_element_type=F32) * factor
    grad_key = jnp.einsum("hqk,qhd->khd", grad_scores, query, preferred_element_type=F32) * factor
    return (grad_query, grad_key, grad_value.astype(BF))


def spread_over_dp(chunks):
    size = chunks.shape[0]
    me = lax.axis_index("dp")
    total = lax.dynamic_index_in_dim(chunks, me, 0, keepdims=False)
    for shift in range(1, size):
        sent = lax.dynamic_index_in_dim(chunks, me ^ shift, 0, keepdims=False)
        total = total + lax.ppermute(sent, "dp", [(i, i ^ shift) for i in range(size)])
    return total


def on_device(
    inputs, teacher, segment, position, wq, wk, wv, wo, wg, wu, wd, q_gain, k_gain, attn_gain, ffn_gain
):
    dp = lax.axis_size("dp")
    tensor = lax.axis_size("tensor")
    ring = Square(tensor) if tensor == 4 else Plain(tensor)
    rows, width = inputs.shape
    share, local_width = wq.shape
    units = wg.shape[1]
    heads_here = local_width // HD
    group = segment.shape[0]
    assert group == LEN and rows * tensor == group

    pieces = local_width // share
    wo_side = jnp.concatenate([wo[i * share : (i + 1) * share] for i in range(pieces)], axis=1)
    attn_shard = jnp.concatenate([wq, wk, wv, wo_side], axis=1)
    attn_all = lax.all_gather(attn_shard, "dp", axis=0, tiled=True)
    pair_all = lax.all_gather(jnp.concatenate([wg, wu], axis=1), "dp", axis=0, tiled=True)
    full_down = lax.all_gather(wd, "dp", axis=1, tiled=True)

    counted = jnp.sum((segment != 0).astype(F32))
    small = jnp.concatenate(
        [
            jnp.stack([q_gain, k_gain, attn_gain, ffn_gain]).astype(F32),
            jnp.broadcast_to(counted, (4, share)),
        ]
    )
    small_all = lax.all_gather(small, "dp", axis=1)
    gains = small_all[:4].reshape(4, width)
    valid_total = jnp.sum(small_all[4, :, 0])
    offset = ring.me * local_width
    gain_qk = lax.dynamic_slice(gains, (0, offset), (2, local_width))
    gain_attn = gains[2]
    gain_ffn = gains[3]

    segment_rel = jnp.take(segment.reshape(tensor, rows), ring.order, axis=0).reshape(group)
    position_rel = jnp.take(position.reshape(tensor, rows), ring.order, axis=0).reshape(group)
    place = (ring.order[:, None] * rows + jnp.arange(rows)[None, :]).reshape(group)
    allowed = (segment_rel[:, None] == segment_rel[None, :]) & (place[:, None] >= place[None, :])
    cosines, sines = tables(position_rel)

    whole_inputs = ring.gather(inputs)
    qkv = attn_all[:, : 3 * local_width]
    full_out = (
        attn_all[:, 3 * local_width :]
        .reshape(dp, share, pieces, share)
        .transpose(2, 1, 0, 3)
        .reshape(local_width, width)
    )
    raw = times(whole_inputs, qkv)
    raw_q = raw[:, :local_width]
    raw_k = raw[:, local_width : 2 * local_width]
    value = raw[:, 2 * local_width :].astype(BF).reshape(group, heads_here, HD)
    squares = ring.total_by_token(jnp.stack([jnp.sum(raw_q * raw_q, axis=1), jnp.sum(raw_k * raw_k, axis=1)]))
    scales = lax.rsqrt(squares / width + EPS)
    scale_q = scales[0][:, None]
    scale_k = scales[1][:, None]
    normed_q = raw_q * scale_q
    normed_k = raw_k * scale_k
    query = rotate(
        (normed_q * gain_qk[0]).reshape(group, heads_here, HD), cosines, sines
    ).astype(BF)
    key = rotate((normed_k * gain_qk[1]).reshape(group, heads_here, HD), cosines, sines).astype(BF)
    mixed, logsum = attend_forward(query, key, value, allowed)
    attn_rows = mixed.reshape(group, local_width)
    branch_attn = ring.scatter(times(attn_rows, full_out))
    scale_attn = lax.rsqrt(jnp.mean(branch_attn * branch_attn, axis=1, keepdims=True) + EPS)
    normed_attn = branch_attn * scale_attn
    resid = inputs.astype(F32) + normed_attn * gain_attn
    whole_h = ring.gather(resid.astype(BF))

    pair = times(whole_h, pair_all)
    gate = pair[:, :units]
    up = pair[:, units:]
    sigma = jax.nn.sigmoid(gate)
    activated = gate * sigma
    hidden = (activated * up).astype(BF)
    branch_ffn = ring.scatter(times(hidden, full_down))
    scale_ffn = lax.rsqrt(jnp.mean(branch_ffn * branch_ffn, axis=1, keepdims=True) + EPS)
    normed_ffn = branch_ffn * scale_ffn
    output = resid + normed_ffn * gain_ffn
    my_segment = lax.dynamic_slice_in_dim(segment, ring.me * rows, rows)
    valid = (my_segment != 0).astype(F32)[:, None]
    error = output - teacher.astype(F32)
    loss_part = jnp.sum(valid * error * error)
    tokens_all = rows * dp * tensor
    grad_output = 2.0 * tokens_all * valid * error / valid_total
    grad_gain_ffn = jnp.sum(grad_output * normed_ffn, axis=0)
    grad_normed = grad_output * gain_ffn
    grad_branch_ffn = (
        scale_ffn
        * (grad_normed - normed_ffn * jnp.mean(grad_normed * normed_ffn, axis=1, keepdims=True))
    ).astype(BF)
    piece = ring.gather(grad_branch_ffn)
    grad_down = inner_rows(hidden, piece).astype(BF)
    sum_down = lax.psum_scatter(grad_down, "dp", scatter_dimension=1, tiled=True)
    grad_hidden = times_transposed(piece, full_down)
    grad_gate = (grad_hidden * up * sigma * (1.0 + gate * (1.0 - sigma))).astype(BF)
    grad_up = (grad_hidden * activated).astype(BF)
    grad_pair = jnp.concatenate([grad_gate, grad_up], axis=1)
    grad_resid = grad_output + ring.scatter(times_transposed(grad_pair, pair_all))
    pair_grads = inner_rows(whole_h, grad_pair).astype(BF)
    sum_pair = lax.psum_scatter(pair_grads, "dp", scatter_dimension=0, tiled=True)
    grad_gain_attn = jnp.sum(grad_resid * normed_attn, axis=0)
    grad_normed = grad_resid * gain_attn
    grad_branch_attn = (
        scale_attn
        * (grad_normed - normed_attn * jnp.mean(grad_normed * normed_attn, axis=1, keepdims=True))
    ).astype(BF)
    piece = ring.gather(grad_branch_attn)
    grad_mixed = times_transposed(piece, full_out).astype(BF).reshape(group, heads_here, HD)
    grad_out_weight = inner_rows(attn_rows, piece).astype(BF)
    sum_out = lax.psum_scatter(grad_out_weight, "dp", scatter_dimension=1, tiled=True)
    grad_query, grad_key, grad_value = attend_backward(query, key, value, allowed, logsum, grad_mixed)
    grad_normed_q = unrotate(grad_query, cosines, sines).reshape(group, local_width)
    grad_normed_k = unrotate(grad_key, cosines, sines).reshape(group, local_width)
    grad_value = grad_value.reshape(group, local_width)
    grad_hat_q = grad_normed_q * gain_qk[0]
    grad_hat_k = grad_normed_k * gain_qk[1]
    inner = ring.total_by_token(
        jnp.stack([jnp.sum(grad_hat_q * normed_q, axis=1), jnp.sum(grad_hat_k * normed_k, axis=1)])
    )
    grad_raw_q = (scale_q * (grad_hat_q - normed_q * (inner[0] / width)[:, None])).astype(BF)
    grad_raw_k = (scale_k * (grad_hat_k - normed_k * (inner[1] / width)[:, None])).astype(BF)
    grad_raw = jnp.concatenate([grad_raw_q, grad_raw_k, grad_value], axis=1)
    qkv_grads = inner_rows(whole_inputs, grad_raw).astype(BF)
    sum_qkv = lax.psum_scatter(qkv_grads, "dp", scatter_dimension=0, tiled=True)
    grad_input = grad_resid + ring.scatter(times_transposed(grad_raw, qkv))

    placed_q = lax.dynamic_update_slice_in_dim(
        jnp.zeros((width,), F32), jnp.sum(grad_normed_q * normed_q, axis=0), offset, 0
    )
    placed_k = lax.dynamic_update_slice_in_dim(
        jnp.zeros((width,), F32), jnp.sum(grad_normed_k * normed_k, axis=0), offset, 0
    )
    late = jnp.stack(
        [placed_q, placed_k, grad_gain_attn, grad_gain_ffn, jnp.broadcast_to(loss_part, (width,))]
    )
    late = jnp.concatenate([late, jnp.zeros((3, width), F32)])
    late = ring.total(late)
    late = spread_over_dp(late.reshape(8, dp, share).transpose(1, 0, 2))
    loss = late[4, 0] / (valid_total * width)

    sum_qkv = sum_qkv.astype(F32)
    sum_pair = sum_pair.astype(F32)
    return (
        output.astype(BF),
        loss,
        grad_input,
        sum_qkv[:, :local_width],
        sum_qkv[:, local_width : 2 * local_width],
        sum_qkv[:, 2 * local_width :],
        sum_out.astype(F32),
        sum_pair[:, :units],
        sum_pair[:, units:],
        sum_down.astype(F32),
        late[0],
        late[1],
        late[2],
        late[3],
    )


def solution(mesh):
    cols = P("dp", "tensor")
    side = P("tensor", "dp")
    both = P(("dp", "tensor"), None)
    one = P("dp")
    return jax.shard_map(
        on_device,
        mesh=mesh,
        in_specs=(both, both, one, one, cols, cols, cols, side, cols, cols, side, one, one, one, one),
        out_specs=(both, P(), both, cols, cols, cols, side, cols, cols, side, one, one, one, one),
        check_vma=False,
    )
```

```python
import jax
import jax.numpy as jnp
from jax import lax
from jax.sharding import PartitionSpec as P


HD = 128
LEN = 1024
EPS = 1e-06
THETA = 500000.0
NEGATIVE = -1e30
BF = jnp.bfloat16
F32 = jnp.float32


def tables(position):
    freq = 1.0 / THETA ** (jnp.arange(0, HD, 2).astype(F32) / HD)
    angle = position.astype(F32)[:, None] * freq[None, :]
    angle = jnp.concatenate([angle, angle], axis=1)[:, None, :]
    return (jnp.cos(angle), jnp.sin(angle))


def rotate(values, cosines, sines):
    half = values.shape[-1] // 2
    turned = jnp.concatenate([-values[..., half:], values[..., :half]], axis=-1)
    return values * cosines + turned * sines


def unrotate(grad, cosines, sines):
    half = grad.shape[-1] // 2
    turned = grad * sines
    return grad * cosines + jnp.concatenate([turned[..., half:], -turned[..., :half]], axis=-1)


def inner_rows(left, right):
    return lax.dot_general(left, right, (((0,), (0,)), ((), ())), preferred_element_type=F32)


def times(left, right):
    return jnp.dot(left, right, preferred_element_type=F32)


def times_transposed(left, right):
    return lax.dot_general(left, right, (((1,), (1,)), ((), ())), preferred_element_type=F32)


def hop(value, way, size=4):
    return lax.ppermute(value, "tensor", [(i, i ^ way) for i in range(size)])


class Square:
    def __init__(self, size):
        self.me = lax.axis_index("tensor")
        self.order = self.me ^ jnp.arange(size)

    def gather(self, own):
        half = own.shape[0] // 2
        across = hop(own, 1)
        along = hop(own, 2)
        first = hop(across[:half], 2)
        second = hop(along[half:], 1)
        return jnp.concatenate([own, across, along, first, second], axis=0)

    def scatter(self, parts):
        rows = parts.shape[0] // 4
        half = rows // 2
        own, across, along, far = (parts[i * rows : (i + 1) * rows] for i in range(4))
        far = far.astype(BF)
        first = hop(far[:half], 1).astype(F32)
        second = hop(far[half:], 2).astype(F32)
        along = jnp.concatenate([along[:half] + first, along[half:]], axis=0).astype(BF)
        across = jnp.concatenate([across[:half], across[half:] + second], axis=0).astype(BF)
        across = hop(across, 1)
        along = hop(along, 2)
        return own + across.astype(F32) + along.astype(F32)

    def total(self, value):
        return (value + hop(value, 1)) + (hop(value, 2) + hop(value, 3))

    def total_by_token(self, value):
        blocks = value.reshape(value.shape[0], 4, -1)
        result = blocks
        for way in (1, 2, 3):
            got = hop(blocks, way)
            result = result + jnp.stack([got[:, r ^ way] for r in range(4)], axis=1)
        return result.reshape(value.shape)


class Plain:
    def __init__(self, size):
        self.me = lax.axis_index("tensor")
        self.order = jnp.arange(size)

    def gather(self, own):
        return lax.all_gather(own, "tensor", axis=0, tiled=True)

    def scatter(self, parts):
        return lax.psum_scatter(
            parts.astype(BF), "tensor", scatter_dimension=0, tiled=True
        ).astype(F32)

    def total(self, value):
        return lax.psum(value, "tensor")

    def total_by_token(self, value):
        return lax.psum(value, "tensor")


def attend_forward(query, key, value, allowed):
    scores = jnp.einsum("qhd,khd->hqk", query, key, preferred_element_type=F32) * HD ** (-0.5)
    scores = jnp.where(allowed[None], scores, NEGATIVE)
    highest = jnp.max(scores, axis=-1, keepdims=True)
    raised = jnp.exp(scores - highest)
    total = jnp.sum(raised, axis=-1, keepdims=True)
    prob = (raised / total).astype(BF)
    mixed = jnp.einsum("hqk,khd->qhd", prob, value, preferred_element_type=F32)
    return (mixed.astype(BF), (highest + jnp.log(total))[..., 0])


def attend_backward(query, key, value, allowed, logsum, grad_mixed):
    scores = jnp.einsum("qhd,khd->hqk", query, key, preferred_element_type=F32) * HD ** (-0.5)
    scores = jnp.where(allowed[None], scores, NEGATIVE)
    prob = jnp.exp(scores - logsum[..., None])
    grad_prob = jnp.einsum("qhd,khd->hqk", grad_mixed, value, preferred_element_type=F32)
    delta = jnp.sum(grad_prob * prob, axis=-1, keepdims=True)
    grad_scores = (prob * (grad_prob - delta)).astype(BF)
    factor = HD ** (-0.5)
    grad_value = jnp.einsum("hqk,qhd->khd", prob.astype(BF), grad_mixed, preferred_element_type=F32)
    grad_query = jnp.einsum("hqk,khd->qhd", grad_scores, key, preferred_element_type=F32) * factor
    grad_key = jnp.einsum("hqk,qhd->khd", grad_scores, query, preferred_element_type=F32) * factor
    return (grad_query, grad_key, grad_value.astype(BF))


def pick_halves(array, axis):
    dp = lax.axis_size("dp")
    first = lax.axis_index("dp") % 2 == 0
    share = array.shape[axis] // dp
    chunks = [lax.slice_in_dim(array, i * share, (i + 1) * share, axis=axis) for i in range(dp)]
    even = jnp.concatenate(chunks[0::2], axis=axis)
    odd = jnp.concatenate(chunks[1::2], axis=axis)
    return jnp.where(first, odd, even), jnp.where(first, even, odd)


def pair_sum(product, sides):
    size = lax.axis_size("dp")
    theirs = product(sides[0]).astype(BF)
    got = lax.ppermute(theirs, "dp", [(i, i ^ 1) for i in range(size)])
    return (product(sides[1]) + got.astype(F32)).astype(BF)


def scatter_pairs(value, axis):
    size = lax.axis_size("dp")
    groups = [list(range(core, size, 2)) for core in (0, 1)]
    return lax.psum_scatter(
        value, "dp", scatter_dimension=axis, axis_index_groups=groups, tiled=True
    )


def spread_over_dp(chunks):
    size = chunks.shape[0]
    me = lax.axis_index("dp")
    total = lax.dynamic_index_in_dim(chunks, me, 0, keepdims=False)
    for shift in range(1, size):
        sent = lax.dynamic_index_in_dim(chunks, me ^ shift, 0, keepdims=False)
        total = total + lax.ppermute(sent, "dp", [(i, i ^ shift) for i in range(size)])
    return total


def layer(
    inputs, teacher, segment, position, wq, wk, wv, wo, wg, wu, wd, q_gain, k_gain, attn_gain, ffn_gain
):
    dp = lax.axis_size("dp")
    tensor = lax.axis_size("tensor")
    ring = Square(tensor) if tensor == 4 else Plain(tensor)
    rows, width = inputs.shape
    share, local_width = wq.shape
    units = wg.shape[1]
    heads_here = local_width // HD
    group = segment.shape[0]
    assert group == LEN and rows * tensor == group

    pieces = local_width // share
    wo_side = jnp.concatenate([wo[i * share : (i + 1) * share] for i in range(pieces)], axis=1)
    attn_shard = jnp.concatenate([wq, wk, wv, wo_side], axis=1)
    attn_all = lax.all_gather(attn_shard, "dp", axis=0, tiled=True)
    pair_all = lax.all_gather(jnp.concatenate([wg, wu], axis=1), "dp", axis=0, tiled=True)
    full_down = lax.all_gather(wd, "dp", axis=1, tiled=True)

    counted = jnp.sum((segment != 0).astype(F32))
    small = jnp.concatenate(
        [
            jnp.stack([q_gain, k_gain, attn_gain, ffn_gain]).astype(F32),
            jnp.broadcast_to(counted, (4, share)),
        ]
    )
    small_all = lax.all_gather(small, "dp", axis=1)
    gains = small_all[:4].reshape(4, width)
    valid_total = jnp.sum(small_all[4, :, 0])
    offset = ring.me * local_width
    gain_qk = lax.dynamic_slice(gains, (0, offset), (2, local_width))
    gain_attn = gains[2]
    gain_ffn = gains[3]

    segment_rel = jnp.take(segment.reshape(tensor, rows), ring.order, axis=0).reshape(group)
    position_rel = jnp.take(position.reshape(tensor, rows), ring.order, axis=0).reshape(group)
    place = (ring.order[:, None] * rows + jnp.arange(rows)[None, :]).reshape(group)
    allowed = (segment_rel[:, None] == segment_rel[None, :]) & (place[:, None] >= place[None, :])
    cosines, sines = tables(position_rel)

    whole_inputs = ring.gather(inputs)
    qkv = attn_all[:, : 3 * local_width]
    full_out = (
        attn_all[:, 3 * local_width :]
        .reshape(dp, share, pieces, share)
        .transpose(2, 1, 0, 3)
        .reshape(local_width, width)
    )
    raw = times(whole_inputs, qkv)
    raw_q = raw[:, :local_width]
    raw_k = raw[:, local_width : 2 * local_width]
    value = raw[:, 2 * local_width :].astype(BF).reshape(group, heads_here, HD)
    squares = ring.total_by_token(jnp.stack([jnp.sum(raw_q * raw_q, axis=1), jnp.sum(raw_k * raw_k, axis=1)]))
    scales = lax.rsqrt(squares / width + EPS)
    scale_q = scales[0][:, None]
    scale_k = scales[1][:, None]
    normed_q = raw_q * scale_q
    normed_k = raw_k * scale_k
    query = rotate(
        (normed_q * gain_qk[0]).reshape(group, heads_here, HD), cosines, sines
    ).astype(BF)
    key = rotate((normed_k * gain_qk[1]).reshape(group, heads_here, HD), cosines, sines).astype(BF)
    mixed, logsum = attend_forward(query, key, value, allowed)
    attn_rows = mixed.reshape(group, local_width)
    branch_attn = ring.scatter(times(attn_rows, full_out))
    scale_attn = lax.rsqrt(jnp.mean(branch_attn * branch_attn, axis=1, keepdims=True) + EPS)
    normed_attn = branch_attn * scale_attn
    resid = inputs.astype(F32) + normed_attn * gain_attn
    whole_h = ring.gather(resid.astype(BF))

    pair = times(whole_h, pair_all)
    gate = pair[:, :units]
    up = pair[:, units:]
    sigma = jax.nn.sigmoid(gate)
    activated = gate * sigma
    hidden = (activated * up).astype(BF)
    branch_ffn = ring.scatter(times(hidden, full_down))
    scale_ffn = lax.rsqrt(jnp.mean(branch_ffn * branch_ffn, axis=1, keepdims=True) + EPS)
    normed_ffn = branch_ffn * scale_ffn
    output = resid + normed_ffn * gain_ffn
    my_segment = lax.dynamic_slice_in_dim(segment, ring.me * rows, rows)
    valid = (my_segment != 0).astype(F32)[:, None]
    error = output - teacher.astype(F32)
    loss_part = jnp.sum(valid * error * error)
    tokens_all = rows * dp * tensor
    grad_output = 2.0 * tokens_all * valid * error / valid_total
    grad_gain_ffn = jnp.sum(grad_output * normed_ffn, axis=0)
    grad_normed = grad_output * gain_ffn
    grad_branch_ffn = (
        scale_ffn
        * (grad_normed - normed_ffn * jnp.mean(grad_normed * normed_ffn, axis=1, keepdims=True))
    ).astype(BF)
    piece = ring.gather(grad_branch_ffn)
    grad_down = pair_sum(lambda side: inner_rows(hidden, side), pick_halves(piece, 1))
    sum_down = scatter_pairs(grad_down, 1)
    piece, grad_down = lax.optimization_barrier((piece, grad_down))
    grad_hidden = times_transposed(piece, full_down)
    grad_gate = (grad_hidden * up * sigma * (1.0 + gate * (1.0 - sigma))).astype(BF)
    grad_up = (grad_hidden * activated).astype(BF)
    grad_pair = jnp.concatenate([grad_gate, grad_up], axis=1)
    back_h = times_transposed(grad_pair, pair_all)
    back_h, grad_pair = lax.optimization_barrier((back_h, grad_pair))
    back_h = ring.scatter(back_h)
    pair_grads = pair_sum(lambda side: inner_rows(side, grad_pair), pick_halves(whole_h, 1))
    sum_pair = scatter_pairs(pair_grads, 0)
    back_h, pair_grads = lax.optimization_barrier((back_h, pair_grads))
    grad_resid = grad_output + back_h
    grad_gain_attn = jnp.sum(grad_resid * normed_attn, axis=0)
    grad_normed = grad_resid * gain_attn
    grad_branch_attn = (
        scale_attn
        * (grad_normed - normed_attn * jnp.mean(grad_normed * normed_attn, axis=1, keepdims=True))
    ).astype(BF)
    piece = ring.gather(grad_branch_attn)
    grad_mixed = times_transposed(piece, full_out).astype(BF).reshape(group, heads_here, HD)
    out_grads = pair_sum(lambda side: inner_rows(attn_rows, side), pick_halves(piece, 1))
    out_grads = (
        out_grads.reshape(pieces, share, dp // 2, share)
        .transpose(2, 1, 0, 3)
        .reshape(dp // 2 * share, pieces * share)
    )
    grad_query, grad_key, grad_value = attend_backward(
        query, key, value, allowed, logsum, grad_mixed
    )
    grad_normed_q = unrotate(grad_query, cosines, sines).reshape(group, local_width)
    grad_normed_k = unrotate(grad_key, cosines, sines).reshape(group, local_width)
    grad_value = grad_value.reshape(group, local_width)
    grad_hat_q = grad_normed_q * gain_qk[0]
    grad_hat_k = grad_normed_k * gain_qk[1]
    inner = ring.total_by_token(
        jnp.stack([jnp.sum(grad_hat_q * normed_q, axis=1), jnp.sum(grad_hat_k * normed_k, axis=1)])
    )
    grad_raw_q = (scale_q * (grad_hat_q - normed_q * (inner[0] / width)[:, None])).astype(BF)
    grad_raw_k = (scale_k * (grad_hat_k - normed_k * (inner[1] / width)[:, None])).astype(BF)
    grad_raw = jnp.concatenate([grad_raw_q, grad_raw_k, grad_value], axis=1)
    qkv_grads = pair_sum(lambda side: inner_rows(side, grad_raw), pick_halves(whole_inputs, 1))
    attn_grads = jnp.concatenate([qkv_grads, out_grads], axis=1)
    sum_attn = scatter_pairs(attn_grads, 0)
    grad_raw, attn_grads = lax.optimization_barrier((grad_raw, attn_grads))
    back_x = times_transposed(grad_raw, qkv)
    grad_input = grad_resid + ring.scatter(back_x)

    placed_q = lax.dynamic_update_slice_in_dim(
        jnp.zeros((width,), F32), jnp.sum(grad_normed_q * normed_q, axis=0), offset, 0
    )
    placed_k = lax.dynamic_update_slice_in_dim(
        jnp.zeros((width,), F32), jnp.sum(grad_normed_k * normed_k, axis=0), offset, 0
    )
    late = jnp.stack(
        [placed_q, placed_k, grad_gain_attn, grad_gain_ffn, jnp.broadcast_to(loss_part, (width,))]
    )
    late = jnp.concatenate([late, jnp.zeros((3, width), F32)])
    late = ring.total(late)
    late = spread_over_dp(late.reshape(8, dp, share).transpose(1, 0, 2))
    loss = late[4, 0] / (valid_total * width)

    sum_attn = sum_attn.astype(F32)
    sum_out = sum_attn[:, 3 * local_width :].reshape(share, pieces, share)
    sum_out = sum_out.transpose(1, 0, 2).reshape(local_width, share)
    sum_pair = sum_pair.astype(F32)
    return (
        output.astype(BF),
        loss,
        grad_input,
        sum_attn[:, :local_width],
        sum_attn[:, local_width : 2 * local_width],
        sum_attn[:, 2 * local_width : 3 * local_width],
        sum_out,
        sum_pair[:, :units],
        sum_pair[:, units:],
        sum_down.astype(F32),
        late[0],
        late[1],
        late[2],
        late[3],
    )


def solution(mesh):
    cols = P("dp", "tensor")
    side = P("tensor", "dp")
    both = P(("dp", "tensor"), None)
    one = P("dp")
    return jax.shard_map(
        layer,
        mesh=mesh,
        in_specs=(both, both, one, one, cols, cols, cols, side, cols, cols, side, one, one, one, one),
        out_specs=(both, P(), both, cols, cols, cols, side, cols, cols, side, one, one, one, one),
        check_vma=False,
    )
```

```python
import jax
import jax.numpy as jnp
from jax import lax
from jax.experimental import pallas as pl
from jax.experimental.pallas import tpu as pltpu
from jax.sharding import PartitionSpec as P


HD = 128
LEN = 1024
EPS = 1e-06
THETA = 500000.0
NEGATIVE = -1e30
BLOCK = 256
BF = jnp.bfloat16
F32 = jnp.float32


def tables(position):
    freq = 1.0 / THETA ** (jnp.arange(0, HD, 2).astype(F32) / HD)
    angle = position.astype(F32)[:, None] * freq[None, :]
    angle = jnp.concatenate([angle, angle], axis=1)[:, None, :]
    return (jnp.cos(angle), jnp.sin(angle))


def rotate(values, cosines, sines):
    half = values.shape[-1] // 2
    turned = jnp.concatenate([-values[..., half:], values[..., :half]], axis=-1)
    return values * cosines + turned * sines


def inner_rows(left, right):
    return lax.dot_general(left, right, (((0,), (0,)), ((), ())), preferred_element_type=F32)


def times(left, right):
    return jnp.dot(left, right, preferred_element_type=F32)


def times_transposed(left, right):
    return lax.dot_general(left, right, (((1,), (1,)), ((), ())), preferred_element_type=F32)


def hop(value, way, size=4):
    return lax.ppermute(value, "tensor", [(i, i ^ way) for i in range(size)])


class Square:
    def __init__(self, size):
        self.size = size
        self.me = lax.axis_index("tensor")
        self.order = self.me ^ jnp.arange(size)

    def gather(self, own):
        half = own.shape[0] // 2
        across = hop(own, 1)
        along = hop(own, 2)
        first = hop(across[:half], 2)
        second = hop(along[half:], 1)
        return jnp.concatenate([own, across, along, first, second], axis=0)

    def scatter(self, parts):
        rows = parts.shape[0] // 4
        half = rows // 2
        own, across, along, far = (parts[i * rows : (i + 1) * rows] for i in range(4))
        far = far.astype(BF)
        first = hop(far[:half], 1).astype(F32)
        second = hop(far[half:], 2).astype(F32)
        along = jnp.concatenate([along[:half] + first, along[half:]], axis=0).astype(BF)
        across = jnp.concatenate([across[:half], across[half:] + second], axis=0).astype(BF)
        across = hop(across, 1)
        along = hop(along, 2)
        return own + across.astype(F32) + along.astype(F32)

    def total(self, value):
        return (value + hop(value, 1)) + (hop(value, 2) + hop(value, 3))

    def total_by_token(self, value):
        blocks = value.reshape(value.shape[0], 4, -1)
        result = blocks
        for way in (1, 2, 3):
            got = hop(blocks, way)
            result = result + jnp.stack([got[:, r ^ way] for r in range(4)], axis=1)
        return result.reshape(value.shape)


class Plain:
    def __init__(self, size):
        self.size = size
        self.me = lax.axis_index("tensor")
        self.order = jnp.arange(size)

    def gather(self, own):
        return lax.all_gather(own, "tensor", axis=0, tiled=True)

    def scatter(self, parts):
        return lax.psum_scatter(
            parts.astype(BF), "tensor", scatter_dimension=0, tiled=True
        ).astype(F32)

    def total(self, value):
        return lax.psum(value, "tensor")

    def total_by_token(self, value):
        return lax.psum(value, "tensor")


def attend_forward(query, key, value, allowed):
    scores = jnp.einsum("qhd,khd->hqk", query, key, preferred_element_type=F32) * HD ** (-0.5)
    scores = jnp.where(allowed[None], scores, NEGATIVE)
    highest = jnp.max(scores, axis=-1, keepdims=True)
    raised = jnp.exp(scores - highest)
    total = jnp.sum(raised, axis=-1, keepdims=True)
    prob = (raised / total).astype(BF)
    mixed = jnp.einsum("hqk,khd->qhd", prob, value, preferred_element_type=F32)
    return (mixed.astype(BF), (highest + jnp.log(total))[..., 0])


def contract(left, right, left_axis, right_axis):
    return lax.dot_general(
        left, right, (((left_axis,), (right_axis,)), ((), ())), preferred_element_type=F32
    )


def cost(flops, *arrays):
    moved = sum(a.size * jnp.dtype(a.dtype).itemsize for a in arrays)
    return pl.CostEstimate(flops=flops, bytes_accessed=moved, transcendentals=0)


def turn_back(grad, cosine, sine):
    return grad * cosine + pltpu.roll(grad * sine, HD // 2, 1)


def attend_backward(query, key, value, grad_mixed, logsum, bias, cosine, sine, block=512):
    group, width = query.shape
    heads = width // HD
    factor = HD ** (-0.5)
    steps = group // block

    def body(q_ref, k_ref, v_ref, g_ref, l_ref, b_ref, c_ref, s_ref, cq_ref, sq_ref, dq_ref, dk_ref, dv_ref, ak, av):
        head = pl.program_id(0)
        step = pl.program_id(1)

        @pl.when(step == 0)
        def _():
            ak[...] = jnp.zeros_like(ak)
            av[...] = jnp.zeros_like(av)

        q = q_ref[...]
        k = k_ref[...]
        g = g_ref[...]
        scores = contract(k, q, 1, 1) * factor + b_ref[...]
        prob = jnp.exp(scores - l_ref[pl.ds(head, 1), :])
        grad_prob = contract(v_ref[...], g, 1, 1)
        delta = jnp.sum(prob * grad_prob, axis=0, keepdims=True)
        grad_scores = (prob * (grad_prob - delta)).astype(BF)
        av[...] += contract(prob.astype(BF), g, 1, 0)
        ak[...] += contract(grad_scores, q, 1, 0)
        dq_ref[...] = turn_back(contract(grad_scores, k, 0, 0) * factor, cq_ref[...], sq_ref[...])

        @pl.when(step == steps - 1)
        def _():
            dk_ref[...] = turn_back(ak[...] * factor, c_ref[...], s_ref[...])
            dv_ref[...] = av[...].astype(BF)

    part = pl.BlockSpec((block, HD), lambda h, i: (i, h))
    whole = pl.BlockSpec((group, HD), lambda h, i: (0, h))
    table = pl.BlockSpec((group, HD), lambda h, i: (0, 0))
    table_part = pl.BlockSpec((block, HD), lambda h, i: (i, 0))
    return pl.pallas_call(
        body,
        grid=(heads, steps),
        in_specs=[
            part, whole, whole, part,
            pl.BlockSpec((heads, block), lambda h, i: (0, i)),
            pl.BlockSpec((group, block), lambda h, i: (0, i)),
            table, table, table_part, table_part,
        ],
        out_specs=[part, whole, whole],
        out_shape=[
            jax.ShapeDtypeStruct((group, width), F32),
            jax.ShapeDtypeStruct((group, width), F32),
            jax.ShapeDtypeStruct((group, width), BF),
        ],
        scratch_shapes=[pltpu.VMEM((group, HD), F32), pltpu.VMEM((group, HD), F32)],
        cost_estimate=cost(10 * group * group * width, bias, query, key, value, grad_mixed),
        name="attend_backward",
    )(query, key, value, grad_mixed, logsum, bias, cosine, sine, cosine, sine)


def pair_backward(piece, down, pair, block=BLOCK):
    group, width = piece.shape
    units = down.shape[0]

    def body(g_ref, w_ref, p_ref, o_ref):
        grad = contract(g_ref[...], w_ref[...], 1, 1)
        gate = p_ref[:, :block]
        up = p_ref[:, block:]
        sigma = 1.0 / (1.0 + jnp.exp(-gate))
        o_ref[:, :block] = (grad * up * sigma * (1.0 + gate * (1.0 - sigma))).astype(BF)
        o_ref[:, block:] = (grad * (gate * sigma)).astype(BF)

    return pl.pallas_call(
        body,
        grid=(units // block,),
        in_specs=[
            pl.BlockSpec((group, width), lambda j: (0, 0)),
            pl.BlockSpec((block, width), lambda j: (j, 0)),
            pl.BlockSpec((group, 2 * block), lambda j: (0, j)),
        ],
        out_specs=pl.BlockSpec((group, 2 * block), lambda j: (0, j)),
        out_shape=jax.ShapeDtypeStruct((group, 2 * units), BF),
        cost_estimate=cost(2 * group * width * units, piece, down, pair),
        compiler_params=pltpu.CompilerParams(vmem_limit_bytes=48 << 20),
        name="pair_backward",
    )(piece, down, pair)


def pair_forward(rows, weights, block=BLOCK):
    group, width = rows.shape
    units = weights.shape[1] // 2

    def body(x_ref, w_ref, p_ref, h_ref):
        both = contract(x_ref[...], w_ref[...], 1, 0)
        p_ref[...] = both
        gate = both[:, :block]
        h_ref[...] = (gate / (1.0 + jnp.exp(-gate)) * both[:, block:]).astype(BF)

    return pl.pallas_call(
        body,
        grid=(units // block,),
        in_specs=[
            pl.BlockSpec((group, width), lambda j: (0, 0)),
            pl.BlockSpec((width, 2 * block), lambda j: (0, j)),
        ],
        out_specs=[
            pl.BlockSpec((group, 2 * block), lambda j: (0, j)),
            pl.BlockSpec((group, block), lambda j: (0, j)),
        ],
        out_shape=[
            jax.ShapeDtypeStruct((group, 2 * units), F32),
            jax.ShapeDtypeStruct((group, units), BF),
        ],
        cost_estimate=cost(4 * group * width * units, rows, weights),
        compiler_params=pltpu.CompilerParams(vmem_limit_bytes=48 << 20),
        name="pair_forward",
    )(rows, weights)


def pick_halves(array, axis):
    dp = lax.axis_size("dp")
    first = lax.axis_index("dp") % 2 == 0
    share = array.shape[axis] // dp
    chunks = [lax.slice_in_dim(array, i * share, (i + 1) * share, axis=axis) for i in range(dp)]
    even = jnp.concatenate(chunks[0::2], axis=axis)
    odd = jnp.concatenate(chunks[1::2], axis=axis)
    return jnp.where(first, odd, even), jnp.where(first, even, odd)


def swap_cores(value):
    return lax.ppermute(value, "dp", [(i, i ^ 1) for i in range(lax.axis_size("dp"))])


def pair_sum(product, sides):
    got = swap_cores(product(sides[0]).astype(BF))
    return (product(sides[1]) + got.astype(F32)).astype(BF)


def interleave(left, right, block):
    count = left.shape[1] // block
    parts = []
    for i in range(count):
        parts += [left[:, i * block : (i + 1) * block], right[:, i * block : (i + 1) * block]]
    return jnp.concatenate(parts, axis=1)


def scatter_pairs(value, axis):
    size = lax.axis_size("dp")
    groups = [list(range(core, size, 2)) for core in (0, 1)]
    return lax.psum_scatter(
        value, "dp", scatter_dimension=axis, axis_index_groups=groups, tiled=True
    )


def spread_over_dp(chunks):
    size = chunks.shape[0]
    me = lax.axis_index("dp")
    total = lax.dynamic_index_in_dim(chunks, me, 0, keepdims=False)
    for shift in range(1, size):
        sent = lax.dynamic_index_in_dim(chunks, me ^ shift, 0, keepdims=False)
        total = total + lax.ppermute(sent, "dp", [(i, i ^ shift) for i in range(size)])
    return total


def layer(
    inputs, teacher, segment, position, wq, wk, wv, wo, wg, wu, wd, q_gain, k_gain, attn_gain, ffn_gain
):
    dp = lax.axis_size("dp")
    tensor = lax.axis_size("tensor")
    ring = Square(tensor) if tensor == 4 else Plain(tensor)
    rows, width = inputs.shape
    share, local_width = wq.shape
    units = wg.shape[1]
    heads_here = local_width // HD
    group = segment.shape[0]
    assert group == LEN and rows * tensor == group

    pieces = local_width // share
    wo_side = jnp.concatenate([wo[i * share : (i + 1) * share] for i in range(pieces)], axis=1)
    attn_shard = jnp.concatenate([wq, wk, wv, wo_side], axis=1)
    attn_all = lax.all_gather(attn_shard, "dp", axis=0, tiled=True)
    pair_all = lax.all_gather(interleave(wg, wu, BLOCK), "dp", axis=0, tiled=True)
    full_down = lax.all_gather(wd, "dp", axis=1, tiled=True)

    counted = jnp.sum((segment != 0).astype(F32))
    small = jnp.concatenate(
        [
            jnp.stack([q_gain, k_gain, attn_gain, ffn_gain]).astype(F32),
            jnp.broadcast_to(counted, (4, share)),
        ]
    )
    small_all = lax.all_gather(small, "dp", axis=1)
    gains = small_all[:4].reshape(4, width)
    valid_total = jnp.sum(small_all[4, :, 0])
    offset = ring.me * local_width
    gain_qk = lax.dynamic_slice(gains, (0, offset), (2, local_width))
    gain_attn = gains[2]
    gain_ffn = gains[3]

    segment_rel = jnp.take(segment.reshape(tensor, rows), ring.order, axis=0).reshape(group)
    position_rel = jnp.take(position.reshape(tensor, rows), ring.order, axis=0).reshape(group)
    place = (ring.order[:, None] * rows + jnp.arange(rows)[None, :]).reshape(group)
    allowed = (segment_rel[:, None] == segment_rel[None, :]) & (place[:, None] >= place[None, :])
    bias = jnp.where(
        (segment_rel[:, None] == segment_rel[None, :]) & (place[:, None] <= place[None, :]), 0.0, NEGATIVE
    )
    cosines, sines = tables(position_rel)
    flat_cosines = cosines[:, 0]
    flat_sines = jnp.concatenate([-sines[:, 0, : HD // 2], sines[:, 0, HD // 2 :]], axis=1)

    whole_inputs = ring.gather(inputs)
    qkv = attn_all[:, : 3 * local_width]
    full_out = (
        attn_all[:, 3 * local_width :]
        .reshape(dp, share, pieces, share)
        .transpose(2, 1, 0, 3)
        .reshape(local_width, width)
    )
    raw = times(whole_inputs, qkv)
    raw_q = raw[:, :local_width]
    raw_k = raw[:, local_width : 2 * local_width]
    value = raw[:, 2 * local_width :].astype(BF)
    squares = ring.total_by_token(jnp.stack([jnp.sum(raw_q * raw_q, axis=1), jnp.sum(raw_k * raw_k, axis=1)]))
    scales = lax.rsqrt(squares / width + EPS)
    scale_q = scales[0][:, None]
    scale_k = scales[1][:, None]
    normed_q = raw_q * scale_q
    normed_k = raw_k * scale_k
    query = rotate(
        (normed_q * gain_qk[0]).reshape(group, heads_here, HD), cosines, sines
    ).astype(BF)
    key = rotate((normed_k * gain_qk[1]).reshape(group, heads_here, HD), cosines, sines).astype(BF)
    mixed, logsum = attend_forward(query, key, value.reshape(group, heads_here, HD), allowed)
    query = query.reshape(group, local_width)
    key = key.reshape(group, local_width)
    attn_rows = mixed.reshape(group, local_width)
    branch_attn = ring.scatter(times(attn_rows, full_out))
    scale_attn = lax.rsqrt(jnp.mean(branch_attn * branch_attn, axis=1, keepdims=True) + EPS)
    normed_attn = branch_attn * scale_attn
    resid = inputs.astype(F32) + normed_attn * gain_attn
    whole_h = ring.gather(resid.astype(BF))

    pair, hidden = pair_forward(whole_h, pair_all)
    branch_ffn = ring.scatter(times(hidden, full_down))
    scale_ffn = lax.rsqrt(jnp.mean(branch_ffn * branch_ffn, axis=1, keepdims=True) + EPS)
    normed_ffn = branch_ffn * scale_ffn
    output = resid + normed_ffn * gain_ffn
    my_segment = lax.dynamic_slice_in_dim(segment, ring.me * rows, rows)
    valid = (my_segment != 0).astype(F32)[:, None]
    error = output - teacher.astype(F32)
    loss_part = jnp.sum(valid * error * error)
    tokens_all = rows * dp * tensor
    grad_output = 2.0 * tokens_all * valid * error / valid_total
    grad_gain_ffn = jnp.sum(grad_output * normed_ffn, axis=0)
    grad_normed = grad_output * gain_ffn
    grad_branch_ffn = (
        scale_ffn
        * (grad_normed - normed_ffn * jnp.mean(grad_normed * normed_ffn, axis=1, keepdims=True))
    ).astype(BF)
    piece = ring.gather(grad_branch_ffn)
    grad_down = pair_sum(lambda side: inner_rows(hidden, side), pick_halves(piece, 1))
    sum_down = scatter_pairs(grad_down, 1)
    piece, grad_down = lax.optimization_barrier((piece, grad_down))
    grad_pair = pair_backward(piece, full_down, pair)
    mine = pick_halves(whole_h, 1)
    theirs = inner_rows(mine[0], grad_pair).astype(BF)
    grad_pair, theirs = lax.optimization_barrier((grad_pair, theirs))
    got = swap_cores(theirs)
    back_h = times_transposed(grad_pair, pair_all)
    back_h, grad_pair = lax.optimization_barrier((back_h, grad_pair))
    back_h = ring.scatter(back_h)
    pair_grads = (inner_rows(mine[1], grad_pair) + got.astype(F32)).astype(BF)
    sum_pair = scatter_pairs(pair_grads, 0)
    back_h, pair_grads = lax.optimization_barrier((back_h, pair_grads))
    grad_resid = grad_output + back_h
    grad_gain_attn = jnp.sum(grad_resid * normed_attn, axis=0)
    grad_normed = grad_resid * gain_attn
    grad_branch_attn = (
        scale_attn
        * (grad_normed - normed_attn * jnp.mean(grad_normed * normed_attn, axis=1, keepdims=True))
    ).astype(BF)
    piece = ring.gather(grad_branch_attn)
    grad_mixed = times_transposed(piece, full_out).astype(BF)
    out_grads = pair_sum(lambda side: inner_rows(attn_rows, side), pick_halves(piece, 1))
    out_grads = (
        out_grads.reshape(pieces, share, dp // 2, share)
        .transpose(2, 1, 0, 3)
        .reshape(dp // 2 * share, pieces * share)
    )
    grad_normed_q, grad_normed_k, grad_value = attend_backward(
        query, key, value, grad_mixed, logsum, bias, flat_cosines, flat_sines
    )
    grad_hat_q = grad_normed_q * gain_qk[0]
    grad_hat_k = grad_normed_k * gain_qk[1]
    inner = ring.total_by_token(
        jnp.stack([jnp.sum(grad_hat_q * normed_q, axis=1), jnp.sum(grad_hat_k * normed_k, axis=1)])
    )
    grad_raw_q = (scale_q * (grad_hat_q - normed_q * (inner[0] / width)[:, None])).astype(BF)
    grad_raw_k = (scale_k * (grad_hat_k - normed_k * (inner[1] / width)[:, None])).astype(BF)
    grad_raw = jnp.concatenate([grad_raw_q, grad_raw_k, grad_value], axis=1)
    qkv_grads = pair_sum(lambda side: inner_rows(side, grad_raw), pick_halves(whole_inputs, 1))
    attn_grads = jnp.concatenate([qkv_grads, out_grads], axis=1)
    sum_attn = scatter_pairs(attn_grads, 0)
    grad_raw, attn_grads = lax.optimization_barrier((grad_raw, attn_grads))
    back_x = times_transposed(grad_raw, qkv)
    grad_input = grad_resid + ring.scatter(back_x)

    placed_q = lax.dynamic_update_slice_in_dim(
        jnp.zeros((width,), F32), jnp.sum(grad_normed_q * normed_q, axis=0), offset, 0
    )
    placed_k = lax.dynamic_update_slice_in_dim(
        jnp.zeros((width,), F32), jnp.sum(grad_normed_k * normed_k, axis=0), offset, 0
    )
    late = jnp.stack(
        [placed_q, placed_k, grad_gain_attn, grad_gain_ffn, jnp.broadcast_to(loss_part, (width,))]
    )
    late = jnp.concatenate([late, jnp.zeros((3, width), F32)])
    late = ring.total(late)
    late = spread_over_dp(late.reshape(8, dp, share).transpose(1, 0, 2))
    loss = late[4, 0] / (valid_total * width)

    sum_attn = sum_attn.astype(F32)
    sum_out = sum_attn[:, 3 * local_width :].reshape(share, pieces, share)
    sum_out = sum_out.transpose(1, 0, 2).reshape(local_width, share)
    sum_pair = sum_pair.astype(F32).reshape(share, units // BLOCK, 2, BLOCK)
    return (
        output.astype(BF),
        loss,
        grad_input,
        sum_attn[:, :local_width],
        sum_attn[:, local_width : 2 * local_width],
        sum_attn[:, 2 * local_width : 3 * local_width],
        sum_out,
        sum_pair[:, :, 0].reshape(share, units),
        sum_pair[:, :, 1].reshape(share, units),
        sum_down.astype(F32),
        late[0],
        late[1],
        late[2],
        late[3],
    )


def solution(mesh):
    cols = P("dp", "tensor")
    side = P("tensor", "dp")
    both = P(("dp", "tensor"), None)
    one = P("dp")
    return jax.shard_map(
        layer,
        mesh=mesh,
        in_specs=(both, both, one, one, cols, cols, cols, side, cols, cols, side, one, one, one, one),
        out_specs=(both, P(), both, cols, cols, cols, side, cols, cols, side, one, one, one, one),
        check_vma=False,
    )
```

```python
import jax
import jax.numpy as jnp
from jax import lax
from jax.experimental import pallas as pl
from jax.experimental.pallas import tpu as pltpu
from jax.sharding import PartitionSpec as P


HD = 128
LEN = 1024
EPS = 1e-06
THETA = 500000.0
NEGATIVE = -1e30
BLOCK = 256
BF = jnp.bfloat16
F32 = jnp.float32


def tables(position):
    freq = 1.0 / THETA ** (jnp.arange(0, HD, 2).astype(F32) / HD)
    angle = position.astype(F32)[:, None] * freq[None, :]
    angle = jnp.concatenate([angle, angle], axis=1)[:, None, :]
    return (jnp.cos(angle), jnp.sin(angle))


def rotate(values, cosines, sines):
    half = values.shape[-1] // 2
    turned = jnp.concatenate([-values[..., half:], values[..., :half]], axis=-1)
    return values * cosines + turned * sines


def inner_rows(left, right):
    return lax.dot_general(left, right, (((0,), (0,)), ((), ())), preferred_element_type=F32)


def times(left, right):
    return jnp.dot(left, right, preferred_element_type=F32)


def times_transposed(left, right):
    return lax.dot_general(left, right, (((1,), (1,)), ((), ())), preferred_element_type=F32)


def hop(value, way, size=4):
    return lax.ppermute(value, "tensor", [(i, i ^ way) for i in range(size)])


class Square:
    def __init__(self, size):
        self.size = size
        self.me = lax.axis_index("tensor")
        self.order = self.me ^ jnp.arange(size)

    def gather_parts(self, own):
        half = own.shape[0] // 2
        across = hop(own, 1)
        along = hop(own, 2)
        first = hop(across[:half], 2)
        second = hop(along[half:], 1)
        return own, across, along, first, second

    def gather(self, own):
        return jnp.concatenate(self.gather_parts(own), axis=0)

    def scatter_product(self, left, right):
        rows = left.shape[0] // 4
        half = rows // 2
        far = times(left[3 * rows :], right).astype(BF)
        first = hop(far[:half], 1)
        second = hop(far[half:], 2)
        near = lax.optimization_barrier(times(left[rows : 3 * rows], right))
        across, along = near[:rows], near[rows:]
        along = jnp.concatenate([along[:half] + first.astype(F32), along[half:]], axis=0).astype(BF)
        across = jnp.concatenate([across[:half], across[half:] + second.astype(F32)], axis=0).astype(BF)
        across = hop(across, 1)
        along = hop(along, 2)
        own = times(left[:rows], right)
        return own, across, along

    def scatter(self, parts):
        rows = parts.shape[0] // 4
        half = rows // 2
        own, across, along, far = (parts[i * rows : (i + 1) * rows] for i in range(4))
        far = far.astype(BF)
        first = hop(far[:half], 1).astype(F32)
        second = hop(far[half:], 2).astype(F32)
        along = jnp.concatenate([along[:half] + first, along[half:]], axis=0).astype(BF)
        across = jnp.concatenate([across[:half], across[half:] + second], axis=0).astype(BF)
        across = hop(across, 1)
        along = hop(along, 2)
        return own + across.astype(F32) + along.astype(F32)

    def total(self, value):
        return (value + hop(value, 1)) + (hop(value, 2) + hop(value, 3))

    def total_by_token(self, value):
        blocks = value.reshape(value.shape[0], 4, -1)
        result = blocks
        for way in (1, 2, 3):
            got = hop(blocks, way)
            result = result + jnp.stack([got[:, r ^ way] for r in range(4)], axis=1)
        return result.reshape(value.shape)


class Plain:
    def __init__(self, size):
        self.size = size
        self.me = lax.axis_index("tensor")
        self.order = jnp.arange(size)

    def gather(self, own):
        return lax.all_gather(own, "tensor", axis=0, tiled=True)

    def scatter_product(self, left, right):
        return (self.scatter(times(left, right)),)

    def scatter(self, parts):
        return lax.psum_scatter(
            parts.astype(BF), "tensor", scatter_dimension=0, tiled=True
        ).astype(F32)

    def total(self, value):
        return lax.psum(value, "tensor")

    def total_by_token(self, value):
        return lax.psum(value, "tensor")


def attend_forward(query, key, value, allowed):
    scores = jnp.einsum("qhd,khd->hqk", query, key, preferred_element_type=F32) * HD ** (-0.5)
    scores = jnp.where(allowed[None], scores, NEGATIVE)
    highest = jnp.max(scores, axis=-1, keepdims=True)
    raised = jnp.exp(scores - highest)
    total = jnp.sum(raised, axis=-1, keepdims=True)
    prob = (raised / total).astype(BF)
    mixed = jnp.einsum("hqk,khd->qhd", prob, value, preferred_element_type=F32)
    return (mixed.astype(BF), (highest + jnp.log(total))[..., 0])


def contract(left, right, left_axis, right_axis):
    return lax.dot_general(
        left, right, (((left_axis,), (right_axis,)), ((), ())), preferred_element_type=F32
    )


def cost(flops, *arrays):
    moved = sum(a.size * jnp.dtype(a.dtype).itemsize for a in arrays)
    return pl.CostEstimate(flops=flops, bytes_accessed=moved, transcendentals=0)


def turn_back(grad, cosine, sine):
    return grad * cosine + pltpu.roll(grad * sine, HD // 2, 1)


def attend_backward(query, key, value, grad_mixed, logsum, bias, cosine, sine, block=512):
    group, width = query.shape
    heads = width // HD
    factor = HD ** (-0.5)
    steps = group // block

    def body(q_ref, k_ref, v_ref, g_ref, l_ref, b_ref, c_ref, s_ref, cq_ref, sq_ref, dq_ref, dk_ref, dv_ref, ak, av):
        head = pl.program_id(0)
        step = pl.program_id(1)

        @pl.when(step == 0)
        def _():
            ak[...] = jnp.zeros_like(ak)
            av[...] = jnp.zeros_like(av)

        q = q_ref[...]
        k = k_ref[...]
        g = g_ref[...]
        scores = contract(k, q, 1, 1) * factor + b_ref[...]
        prob = jnp.exp(scores - l_ref[pl.ds(head, 1), :])
        grad_prob = contract(v_ref[...], g, 1, 1)
        delta = jnp.sum(prob * grad_prob, axis=0, keepdims=True)
        grad_scores = (prob * (grad_prob - delta)).astype(BF)
        av[...] += contract(prob.astype(BF), g, 1, 0)
        ak[...] += contract(grad_scores, q, 1, 0)
        dq_ref[...] = turn_back(contract(grad_scores, k, 0, 0) * factor, cq_ref[...], sq_ref[...])

        @pl.when(step == steps - 1)
        def _():
            dk_ref[...] = turn_back(ak[...] * factor, c_ref[...], s_ref[...])
            dv_ref[...] = av[...].astype(BF)

    part = pl.BlockSpec((block, HD), lambda h, i: (i, h))
    whole = pl.BlockSpec((group, HD), lambda h, i: (0, h))
    table = pl.BlockSpec((group, HD), lambda h, i: (0, 0))
    table_part = pl.BlockSpec((block, HD), lambda h, i: (i, 0))
    return pl.pallas_call(
        body,
        grid=(heads, steps),
        in_specs=[
            part, whole, whole, part,
            pl.BlockSpec((heads, block), lambda h, i: (0, i)),
            pl.BlockSpec((group, block), lambda h, i: (0, i)),
            table, table, table_part, table_part,
        ],
        out_specs=[part, whole, whole],
        out_shape=[
            jax.ShapeDtypeStruct((group, width), F32),
            jax.ShapeDtypeStruct((group, width), F32),
            jax.ShapeDtypeStruct((group, width), BF),
        ],
        scratch_shapes=[pltpu.VMEM((group, HD), F32), pltpu.VMEM((group, HD), F32)],
        cost_estimate=cost(10 * group * group * width, bias, query, key, value, grad_mixed),
        name="attend_backward",
    )(query, key, value, grad_mixed, logsum, bias, cosine, sine, cosine, sine)


def pair_backward(piece, down, pair, block=BLOCK):
    group, width = piece.shape
    units = down.shape[0]

    def body(g_ref, w_ref, p_ref, o_ref):
        grad = contract(g_ref[...], w_ref[...], 1, 1)
        gate = p_ref[:, :block]
        up = p_ref[:, block:]
        sigma = 1.0 / (1.0 + jnp.exp(-gate))
        o_ref[:, :block] = (grad * up * sigma * (1.0 + gate * (1.0 - sigma))).astype(BF)
        o_ref[:, block:] = (grad * (gate * sigma)).astype(BF)

    return pl.pallas_call(
        body,
        grid=(units // block,),
        in_specs=[
            pl.BlockSpec((group, width), lambda j: (0, 0)),
            pl.BlockSpec((block, width), lambda j: (j, 0)),
            pl.BlockSpec((group, 2 * block), lambda j: (0, j)),
        ],
        out_specs=pl.BlockSpec((group, 2 * block), lambda j: (0, j)),
        out_shape=jax.ShapeDtypeStruct((group, 2 * units), BF),
        cost_estimate=cost(2 * group * width * units, piece, down, pair),
        compiler_params=pltpu.CompilerParams(vmem_limit_bytes=48 << 20),
        name="pair_backward",
    )(piece, down, pair)


def loss_and_back(parts, resid, teacher, valid, gain, block=64):
    rows, width = resid.shape
    count = len(parts)

    def body(*refs):
        x_ref, t_ref, v_ref, w_ref, o_ref, g_ref, b_ref, sum_ref = refs[count:]
        branch = refs[0][...]
        for ref in refs[1:count]:
            branch = branch + ref[...].astype(F32)
        scale = lax.rsqrt(jnp.mean(branch * branch, axis=1, keepdims=True) + EPS)
        normed = branch * scale
        out = x_ref[...] + normed * w_ref[...]
        o_ref[...] = out.astype(BF)
        error = out - t_ref[...].astype(F32)
        grad = error * v_ref[:, 1:2]
        g_ref[...] = grad
        back = grad * w_ref[...]
        inner = jnp.mean(back * normed, axis=1, keepdims=True)
        b_ref[...] = (scale * (back - normed * inner)).astype(BF)

        @pl.when(pl.program_id(0) == 0)
        def _():
            sum_ref[...] = jnp.zeros_like(sum_ref)

        sum_ref[0:1, :] += jnp.sum(grad * normed, axis=0, keepdims=True)
        sum_ref[1:2, :] += jnp.sum(error * error * v_ref[:, 0:1], axis=0, keepdims=True)

    row = pl.BlockSpec((block, width), lambda i: (i, 0))
    arrays = (*parts, resid, teacher)
    return pl.pallas_call(
        body,
        grid=(rows // block,),
        in_specs=[row] * len(arrays)
        + [pl.BlockSpec((block, 2), lambda i: (i, 0)), pl.BlockSpec((1, width), lambda i: (0, 0))],
        out_specs=[row, row, row, pl.BlockSpec((8, width), lambda i: (0, 0))],
        out_shape=[
            jax.ShapeDtypeStruct((rows, width), BF),
            jax.ShapeDtypeStruct((rows, width), F32),
            jax.ShapeDtypeStruct((rows, width), BF),
            jax.ShapeDtypeStruct((8, width), F32),
        ],
        cost_estimate=cost(30 * rows * width, *arrays),
        name="loss_and_back",
    )(*arrays, valid, gain.reshape(1, width))


def pair_forward(rows, weights, block=BLOCK):
    group, width = rows.shape
    units = weights.shape[1] // 2

    def body(x_ref, w_ref, p_ref, h_ref):
        both = contract(x_ref[...], w_ref[...], 1, 0)
        p_ref[...] = both
        gate = both[:, :block]
        h_ref[...] = (gate / (1.0 + jnp.exp(-gate)) * both[:, block:]).astype(BF)

    return pl.pallas_call(
        body,
        grid=(units // block,),
        in_specs=[
            pl.BlockSpec((group, width), lambda j: (0, 0)),
            pl.BlockSpec((width, 2 * block), lambda j: (0, j)),
        ],
        out_specs=[
            pl.BlockSpec((group, 2 * block), lambda j: (0, j)),
            pl.BlockSpec((group, block), lambda j: (0, j)),
        ],
        out_shape=[
            jax.ShapeDtypeStruct((group, 2 * units), F32),
            jax.ShapeDtypeStruct((group, units), BF),
        ],
        cost_estimate=cost(4 * group * width * units, rows, weights),
        compiler_params=pltpu.CompilerParams(vmem_limit_bytes=48 << 20),
        name="pair_forward",
    )(rows, weights)


def pick_halves(array, axis):
    dp = lax.axis_size("dp")
    first = lax.axis_index("dp") % 2 == 0
    share = array.shape[axis] // dp
    chunks = [lax.slice_in_dim(array, i * share, (i + 1) * share, axis=axis) for i in range(dp)]
    even = jnp.concatenate(chunks[0::2], axis=axis)
    odd = jnp.concatenate(chunks[1::2], axis=axis)
    return jnp.where(first, odd, even), jnp.where(first, even, odd)


def swap_cores(value):
    return lax.ppermute(value, "dp", [(i, i ^ 1) for i in range(lax.axis_size("dp"))])


def pair_sum(product, sides):
    got = swap_cores(product(sides[0]).astype(BF))
    return (product(sides[1]) + got.astype(F32)).astype(BF)


def interleave(left, right, block):
    count = left.shape[1] // block
    parts = []
    for i in range(count):
        parts += [left[:, i * block : (i + 1) * block], right[:, i * block : (i + 1) * block]]
    return jnp.concatenate(parts, axis=1)


def scatter_pairs(value, axis):
    size = lax.axis_size("dp")
    groups = [list(range(core, size, 2)) for core in (0, 1)]
    return lax.psum_scatter(
        value, "dp", scatter_dimension=axis, axis_index_groups=groups, tiled=True
    )


def spread_over_dp(chunks):
    size = chunks.shape[0]
    me = lax.axis_index("dp")
    total = lax.dynamic_index_in_dim(chunks, me, 0, keepdims=False)
    for shift in range(1, size):
        sent = lax.dynamic_index_in_dim(chunks, me ^ shift, 0, keepdims=False)
        total = total + lax.ppermute(sent, "dp", [(i, i ^ shift) for i in range(size)])
    return total


def layer(
    inputs, teacher, segment, position, wq, wk, wv, wo, wg, wu, wd, q_gain, k_gain, attn_gain, ffn_gain
):
    dp = lax.axis_size("dp")
    tensor = lax.axis_size("tensor")
    ring = Square(tensor) if tensor == 4 else Plain(tensor)
    rows, width = inputs.shape
    share, local_width = wq.shape
    units = wg.shape[1]
    heads_here = local_width // HD
    group = segment.shape[0]
    assert group == LEN and rows * tensor == group

    pieces = local_width // share
    wo_side = jnp.concatenate([wo[i * share : (i + 1) * share] for i in range(pieces)], axis=1)
    attn_shard = jnp.concatenate([wq, wk, wv, wo_side], axis=1)
    attn_all = lax.all_gather(attn_shard, "dp", axis=0, tiled=True)
    pair_all = lax.all_gather(interleave(wg, wu, BLOCK), "dp", axis=0, tiled=True)
    full_down = lax.all_gather(wd, "dp", axis=1, tiled=True)

    counted = jnp.sum((segment != 0).astype(F32))
    small = jnp.concatenate(
        [
            jnp.stack([q_gain, k_gain, attn_gain, ffn_gain]).astype(F32),
            jnp.broadcast_to(counted, (4, share)),
        ]
    )
    small_all = lax.all_gather(small, "dp", axis=1)
    gains = small_all[:4].reshape(4, width)
    valid_total = jnp.sum(small_all[4, :, 0])
    offset = ring.me * local_width
    gain_qk = lax.dynamic_slice(gains, (0, offset), (2, local_width))
    gain_attn = gains[2]
    gain_ffn = gains[3]

    segment_rel = jnp.take(segment.reshape(tensor, rows), ring.order, axis=0).reshape(group)
    position_rel = jnp.take(position.reshape(tensor, rows), ring.order, axis=0).reshape(group)
    place = (ring.order[:, None] * rows + jnp.arange(rows)[None, :]).reshape(group)
    allowed = (segment_rel[:, None] == segment_rel[None, :]) & (place[:, None] >= place[None, :])
    bias = jnp.where(
        (segment_rel[:, None] == segment_rel[None, :]) & (place[:, None] <= place[None, :]), 0.0, NEGATIVE
    )
    cosines, sines = tables(position_rel)
    flat_cosines = cosines[:, 0]
    flat_sines = jnp.concatenate([-sines[:, 0, : HD // 2], sines[:, 0, HD // 2 :]], axis=1)

    whole_inputs = ring.gather(inputs)
    qkv = attn_all[:, : 3 * local_width]
    full_out = (
        attn_all[:, 3 * local_width :]
        .reshape(dp, share, pieces, share)
        .transpose(2, 1, 0, 3)
        .reshape(local_width, width)
    )
    raw = times(whole_inputs, qkv)
    raw_q = raw[:, :local_width]
    raw_k = raw[:, local_width : 2 * local_width]
    value = raw[:, 2 * local_width :].astype(BF)
    squares = ring.total_by_token(jnp.stack([jnp.sum(raw_q * raw_q, axis=1), jnp.sum(raw_k * raw_k, axis=1)]))
    scales = lax.rsqrt(squares / width + EPS)
    scale_q = scales[0][:, None]
    scale_k = scales[1][:, None]
    normed_q = raw_q * scale_q
    normed_k = raw_k * scale_k
    query = rotate(
        (normed_q * gain_qk[0]).reshape(group, heads_here, HD), cosines, sines
    ).astype(BF)
    key = rotate((normed_k * gain_qk[1]).reshape(group, heads_here, HD), cosines, sines).astype(BF)
    mixed, logsum = attend_forward(query, key, value.reshape(group, heads_here, HD), allowed)
    query = query.reshape(group, local_width)
    key = key.reshape(group, local_width)
    attn_rows = mixed.reshape(group, local_width)
    branch_attn = ring.scatter(times(attn_rows, full_out))
    scale_attn = lax.rsqrt(jnp.mean(branch_attn * branch_attn, axis=1, keepdims=True) + EPS)
    normed_attn = branch_attn * scale_attn
    resid = inputs.astype(F32) + normed_attn * gain_attn
    whole_h = ring.gather(resid.astype(BF))

    pair, hidden = pair_forward(whole_h, pair_all)
    my_segment = lax.dynamic_slice_in_dim(segment, ring.me * rows, rows)
    valid = (my_segment != 0).astype(F32)
    valid = jnp.stack([valid, valid * (2.0 * (rows * dp * tensor) / valid_total)], axis=1)
    parts = ring.scatter_product(hidden, full_down)
    output, grad_output, grad_branch_ffn, sums = loss_and_back(
        parts, resid, teacher, valid, gain_ffn
    )
    grad_gain_ffn = sums[0]
    loss_part = jnp.sum(sums[1])
    if tensor == 4:
        got_rows = ring.gather_parts(grad_branch_ffn)
        cut = 3 * rows
        near_halves = pick_halves(jnp.concatenate(got_rows[:3], axis=0), 1)
        far_halves = pick_halves(jnp.concatenate(got_rows[3:], axis=0), 1)
        near = lax.optimization_barrier(
            tuple(inner_rows(hidden[:cut], half) for half in near_halves)
        )
        theirs = (near[0] + inner_rows(hidden[cut:], far_halves[0])).astype(BF)
        got = swap_cores(theirs)
        grad_down = near[1] + inner_rows(hidden[cut:], far_halves[1])
        grad_down = (grad_down + got.astype(F32)).astype(BF)
        piece = jnp.concatenate(got_rows, axis=0)
    else:
        piece = ring.gather(grad_branch_ffn)
        grad_down = pair_sum(lambda side: inner_rows(hidden, side), pick_halves(piece, 1))
    sum_down = scatter_pairs(grad_down, 1)
    piece, grad_down = lax.optimization_barrier((piece, grad_down))
    grad_pair = pair_backward(piece, full_down, pair)
    mine = pick_halves(whole_h, 1)
    theirs = inner_rows(mine[0], grad_pair).astype(BF)
    grad_pair, theirs = lax.optimization_barrier((grad_pair, theirs))
    got = swap_cores(theirs)
    back_h = times_transposed(grad_pair, pair_all)
    back_h, grad_pair = lax.optimization_barrier((back_h, grad_pair))
    back_h = ring.scatter(back_h)
    pair_grads = (inner_rows(mine[1], grad_pair) + got.astype(F32)).astype(BF)
    sum_pair = scatter_pairs(pair_grads, 0)
    back_h, pair_grads = lax.optimization_barrier((back_h, pair_grads))
    grad_resid = grad_output + back_h
    grad_gain_attn = jnp.sum(grad_resid * normed_attn, axis=0)
    grad_normed = grad_resid * gain_attn
    grad_branch_attn = (
        scale_attn
        * (grad_normed - normed_attn * jnp.mean(grad_normed * normed_attn, axis=1, keepdims=True))
    ).astype(BF)
    piece = ring.gather(grad_branch_attn)
    grad_mixed = times_transposed(piece, full_out).astype(BF)
    out_grads = pair_sum(lambda side: inner_rows(attn_rows, side), pick_halves(piece, 1))
    out_grads = (
        out_grads.reshape(pieces, share, dp // 2, share)
        .transpose(2, 1, 0, 3)
        .reshape(dp // 2 * share, pieces * share)
    )
    grad_normed_q, grad_normed_k, grad_value = attend_backward(
        query, key, value, grad_mixed, logsum, bias, flat_cosines, flat_sines
    )
    grad_hat_q = grad_normed_q * gain_qk[0]
    grad_hat_k = grad_normed_k * gain_qk[1]
    inner = ring.total_by_token(
        jnp.stack([jnp.sum(grad_hat_q * normed_q, axis=1), jnp.sum(grad_hat_k * normed_k, axis=1)])
    )
    grad_raw_q = (scale_q * (grad_hat_q - normed_q * (inner[0] / width)[:, None])).astype(BF)
    grad_raw_k = (scale_k * (grad_hat_k - normed_k * (inner[1] / width)[:, None])).astype(BF)
    grad_raw = jnp.concatenate([grad_raw_q, grad_raw_k, grad_value], axis=1)
    qkv_grads = pair_sum(lambda side: inner_rows(side, grad_raw), pick_halves(whole_inputs, 1))
    attn_grads = jnp.concatenate([qkv_grads, out_grads], axis=1)
    sum_attn = scatter_pairs(attn_grads, 0)
    grad_raw, attn_grads = lax.optimization_barrier((grad_raw, attn_grads))
    back_x = times_transposed(grad_raw, qkv)
    grad_input = grad_resid + ring.scatter(back_x)

    placed_q = lax.dynamic_update_slice_in_dim(
        jnp.zeros((width,), F32), jnp.sum(grad_normed_q * normed_q, axis=0), offset, 0
    )
    placed_k = lax.dynamic_update_slice_in_dim(
        jnp.zeros((width,), F32), jnp.sum(grad_normed_k * normed_k, axis=0), offset, 0
    )
    late = jnp.stack(
        [placed_q, placed_k, grad_gain_attn, grad_gain_ffn, jnp.broadcast_to(loss_part, (width,))]
    )
    late = jnp.concatenate([late, jnp.zeros((3, width), F32)])
    late = ring.total(late)
    late = spread_over_dp(late.reshape(8, dp, share).transpose(1, 0, 2))
    loss = late[4, 0] / (valid_total * width)

    sum_attn = sum_attn.astype(F32)
    sum_out = sum_attn[:, 3 * local_width :].reshape(share, pieces, share)
    sum_out = sum_out.transpose(1, 0, 2).reshape(local_width, share)
    sum_pair = sum_pair.astype(F32).reshape(share, units // BLOCK, 2, BLOCK)
    return (
        output,
        loss,
        grad_input,
        sum_attn[:, :local_width],
        sum_attn[:, local_width : 2 * local_width],
        sum_attn[:, 2 * local_width : 3 * local_width],
        sum_out,
        sum_pair[:, :, 0].reshape(share, units),
        sum_pair[:, :, 1].reshape(share, units),
        sum_down.astype(F32),
        late[0],
        late[1],
        late[2],
        late[3],
    )


def solution(mesh):
    cols = P("dp", "tensor")
    side = P("tensor", "dp")
    both = P(("dp", "tensor"), None)
    one = P("dp")
    return jax.shard_map(
        layer,
        mesh=mesh,
        in_specs=(both, both, one, one, cols, cols, cols, side, cols, cols, side, one, one, one, one),
        out_specs=(both, P(), both, cols, cols, cols, side, cols, cols, side, one, one, one, one),
        check_vma=False,
    )
```

```python
import jax
import jax.numpy as jnp
from jax import lax
from jax.experimental import pallas as pl
from jax.experimental.pallas import tpu as pltpu
from jax.sharding import PartitionSpec as P


HD = 128
LEN = 1024
EPS = 1e-06
THETA = 500000.0
NEGATIVE = -1e30
BLOCK = 256
BF = jnp.bfloat16
F32 = jnp.float32


def tables(position):
    freq = 1.0 / THETA ** (jnp.arange(0, HD, 2).astype(F32) / HD)
    angle = position.astype(F32)[:, None] * freq[None, :]
    angle = jnp.concatenate([angle, angle], axis=1)[:, None, :]
    return (jnp.cos(angle), jnp.sin(angle))


def rotate(values, cosines, sines):
    half = values.shape[-1] // 2
    turned = jnp.concatenate([-values[..., half:], values[..., :half]], axis=-1)
    return values * cosines + turned * sines


def inner_rows(left, right):
    return lax.dot_general(left, right, (((0,), (0,)), ((), ())), preferred_element_type=F32)


def times(left, right):
    return jnp.dot(left, right, preferred_element_type=F32)


def times_transposed(left, right):
    return lax.dot_general(left, right, (((1,), (1,)), ((), ())), preferred_element_type=F32)


def hop(value, way, size=4):
    return lax.ppermute(value, "tensor", [(i, i ^ way) for i in range(size)])


class Square:
    def __init__(self, size):
        self.size = size
        self.me = lax.axis_index("tensor")
        self.order = self.me ^ jnp.arange(size)

    def gather_halves(self, upper, lower):
        across_a = hop(upper, 1)
        along_a = hop(upper, 2)
        across_b = hop(lower, 1)
        along_b = hop(lower, 2)
        first = hop(across_a, 2)
        second = hop(along_b, 1)
        return upper, lower, across_a, across_b, along_a, along_b, first, second

    def gather(self, own):
        half = own.shape[0] // 2
        across = hop(own, 1)
        along = hop(own, 2)
        first = hop(across[:half], 2)
        second = hop(along[half:], 1)
        return jnp.concatenate([own, across, along, first, second], axis=0)

    def scatter_product(self, left, right):
        rows = left.shape[0] // 4
        half = rows // 2
        far = times(left[3 * rows :], right).astype(BF)
        first = hop(far[:half], 1)
        second = hop(far[half:], 2)
        near = lax.optimization_barrier(times(left[rows : 3 * rows], right))
        across_a = hop(near[:half].astype(BF), 1)
        along_a = hop((near[rows : rows + half] + first.astype(F32)).astype(BF), 2)
        across_b = hop((near[half:rows] + second.astype(F32)).astype(BF), 1)
        along_b = hop(near[rows + half :].astype(BF), 2)
        own = times(left[:rows], right)
        return own, (across_a, along_a), (across_b, along_b)

    def scatter(self, parts):
        rows = parts.shape[0] // 4
        half = rows // 2
        own, across, along, far = (parts[i * rows : (i + 1) * rows] for i in range(4))
        far = far.astype(BF)
        first = hop(far[:half], 1).astype(F32)
        second = hop(far[half:], 2).astype(F32)
        along = jnp.concatenate([along[:half] + first, along[half:]], axis=0).astype(BF)
        across = jnp.concatenate([across[:half], across[half:] + second], axis=0).astype(BF)
        across = hop(across, 1)
        along = hop(along, 2)
        return own + across.astype(F32) + along.astype(F32)

    def total(self, value):
        return (value + hop(value, 1)) + (hop(value, 2) + hop(value, 3))

    def total_by_token(self, value):
        blocks = value.reshape(value.shape[0], 4, -1)
        result = blocks
        for way in (1, 2, 3):
            got = hop(blocks, way)
            result = result + jnp.stack([got[:, r ^ way] for r in range(4)], axis=1)
        return result.reshape(value.shape)


class Plain:
    def __init__(self, size):
        self.size = size
        self.me = lax.axis_index("tensor")
        self.order = jnp.arange(size)

    def gather(self, own):
        return lax.all_gather(own, "tensor", axis=0, tiled=True)

    def scatter_product(self, left, right):
        return self.scatter(times(left, right))

    def scatter(self, parts):
        return lax.psum_scatter(
            parts.astype(BF), "tensor", scatter_dimension=0, tiled=True
        ).astype(F32)

    def total(self, value):
        return lax.psum(value, "tensor")

    def total_by_token(self, value):
        return lax.psum(value, "tensor")


def attend_forward(query, key, value, allowed):
    scores = jnp.einsum("qhd,khd->hqk", query, key, preferred_element_type=F32) * HD ** (-0.5)
    scores = jnp.where(allowed[None], scores, NEGATIVE)
    highest = jnp.max(scores, axis=-1, keepdims=True)
    raised = jnp.exp(scores - highest)
    total = jnp.sum(raised, axis=-1, keepdims=True)
    prob = (raised / total).astype(BF)
    mixed = jnp.einsum("hqk,khd->qhd", prob, value, preferred_element_type=F32)
    return (mixed.astype(BF), (highest + jnp.log(total))[..., 0])


def contract(left, right, left_axis, right_axis):
    return lax.dot_general(
        left, right, (((left_axis,), (right_axis,)), ((), ())), preferred_element_type=F32
    )


def cost(flops, *arrays):
    moved = sum(a.size * jnp.dtype(a.dtype).itemsize for a in arrays)
    return pl.CostEstimate(flops=flops, bytes_accessed=moved, transcendentals=0)


def turn_back(grad, cosine, sine):
    return grad * cosine + pltpu.roll(grad * sine, HD // 2, 1)


def attend_backward(query, key, value, grad_mixed, logsum, bias, cosine, sine, block=512):
    group, width = query.shape
    heads = width // HD
    factor = HD ** (-0.5)
    steps = group // block

    def body(q_ref, k_ref, v_ref, g_ref, l_ref, b_ref, c_ref, s_ref, cq_ref, sq_ref, dq_ref, dk_ref, dv_ref, ak, av):
        head = pl.program_id(0)
        step = pl.program_id(1)

        @pl.when(step == 0)
        def _():
            ak[...] = jnp.zeros_like(ak)
            av[...] = jnp.zeros_like(av)

        q = q_ref[...]
        k = k_ref[...]
        g = g_ref[...]
        scores = contract(k, q, 1, 1) * factor + b_ref[...]
        prob = jnp.exp(scores - l_ref[pl.ds(head, 1), :])
        grad_prob = contract(v_ref[...], g, 1, 1)
        delta = jnp.sum(prob * grad_prob, axis=0, keepdims=True)
        grad_scores = (prob * (grad_prob - delta)).astype(BF)
        av[...] += contract(prob.astype(BF), g, 1, 0)
        ak[...] += contract(grad_scores, q, 1, 0)
        dq_ref[...] = turn_back(contract(grad_scores, k, 0, 0) * factor, cq_ref[...], sq_ref[...])

        @pl.when(step == steps - 1)
        def _():
            dk_ref[...] = turn_back(ak[...] * factor, c_ref[...], s_ref[...])
            dv_ref[...] = av[...].astype(BF)

    part = pl.BlockSpec((block, HD), lambda h, i: (i, h))
    whole = pl.BlockSpec((group, HD), lambda h, i: (0, h))
    table = pl.BlockSpec((group, HD), lambda h, i: (0, 0))
    table_part = pl.BlockSpec((block, HD), lambda h, i: (i, 0))
    return pl.pallas_call(
        body,
        grid=(heads, steps),
        in_specs=[
            part, whole, whole, part,
            pl.BlockSpec((heads, block), lambda h, i: (0, i)),
            pl.BlockSpec((group, block), lambda h, i: (0, i)),
            table, table, table_part, table_part,
        ],
        out_specs=[part, whole, whole],
        out_shape=[
            jax.ShapeDtypeStruct((group, width), F32),
            jax.ShapeDtypeStruct((group, width), F32),
            jax.ShapeDtypeStruct((group, width), BF),
        ],
        scratch_shapes=[pltpu.VMEM((group, HD), F32), pltpu.VMEM((group, HD), F32)],
        cost_estimate=cost(10 * group * group * width, bias, query, key, value, grad_mixed),
        name="attend_backward",
    )(query, key, value, grad_mixed, logsum, bias, cosine, sine, cosine, sine)


def pair_backward(piece, down, pair, block=BLOCK):
    group, width = piece.shape
    units = down.shape[0]

    def body(g_ref, w_ref, p_ref, o_ref):
        grad = contract(g_ref[...], w_ref[...], 1, 1)
        gate = p_ref[:, :block]
        up = p_ref[:, block:]
        sigma = 1.0 / (1.0 + jnp.exp(-gate))
        o_ref[:, :block] = (grad * up * sigma * (1.0 + gate * (1.0 - sigma))).astype(BF)
        o_ref[:, block:] = (grad * (gate * sigma)).astype(BF)

    return pl.pallas_call(
        body,
        grid=(units // block,),
        in_specs=[
            pl.BlockSpec((group, width), lambda j: (0, 0)),
            pl.BlockSpec((block, width), lambda j: (j, 0)),
            pl.BlockSpec((group, 2 * block), lambda j: (0, j)),
        ],
        out_specs=pl.BlockSpec((group, 2 * block), lambda j: (0, j)),
        out_shape=jax.ShapeDtypeStruct((group, 2 * units), BF),
        cost_estimate=cost(2 * group * width * units, piece, down, pair),
        compiler_params=pltpu.CompilerParams(vmem_limit_bytes=48 << 20),
        name="pair_backward",
    )(piece, down, pair)


def loss_and_back(own, arrived, resid, teacher, valid, gain, first, last, kept=None, block=64):
    rows, width = resid.shape
    count = len(arrived)
    held = () if kept is None else tuple(kept)

    def body(*refs):
        own_ref, x_ref, t_ref, v_ref, w_ref = refs[:5]
        o_ref, g_ref, b_ref, sum_ref = refs[5 + count + len(held) :]
        branch = own_ref[...]
        for ref in refs[5 : 5 + count]:
            branch = branch + ref[...].astype(F32)
        scale = lax.rsqrt(jnp.mean(branch * branch, axis=1, keepdims=True) + EPS)
        normed = branch * scale
        out = x_ref[...] + normed * w_ref[...]
        o_ref[...] = out.astype(BF)
        error = out - t_ref[...].astype(F32)
        grad = error * v_ref[:, 1:2]
        g_ref[...] = grad
        back = grad * w_ref[...]
        inner = jnp.mean(back * normed, axis=1, keepdims=True)
        b_ref[...] = (scale * (back - normed * inner)).astype(BF)

        @pl.when(pl.program_id(0) == 0)
        def _():
            sum_ref[...] = jnp.zeros_like(sum_ref)

        sum_ref[0:1, :] += jnp.sum(grad * normed, axis=0, keepdims=True)
        sum_ref[1:2, :] += jnp.sum(error * error * v_ref[:, 0:1], axis=0, keepdims=True)

    skip = first // block
    row = pl.BlockSpec((block, width), lambda i: (i + skip, 0))
    part = pl.BlockSpec((block, width), lambda i: (i, 0))
    arrays = (own, resid, teacher)
    return pl.pallas_call(
        body,
        grid=((last - first) // block,),
        in_specs=[row] * 3
        + [
            pl.BlockSpec((block, 2), lambda i: (i + skip, 0)),
            pl.BlockSpec((1, width), lambda i: (0, 0)),
        ]
        + [part] * count
        + [pl.BlockSpec(memory_space=pl.ANY)] * len(held),
        out_specs=[row, row, part, pl.BlockSpec((8, width), lambda i: (0, 0))],
        out_shape=[
            jax.ShapeDtypeStruct((rows, width), BF),
            jax.ShapeDtypeStruct((rows, width), F32),
            jax.ShapeDtypeStruct((last - first, width), BF),
            jax.ShapeDtypeStruct((8, width), F32),
        ],
        input_output_aliases={5 + count + i: i for i in range(len(held))},
        cost_estimate=cost(30 * (last - first) * width, *arrived, *arrived),
        name="loss_and_back",
    )(*arrays, valid, gain.reshape(1, width), *arrived, *held)


def pair_forward(rows, weights, block=BLOCK):
    group, width = rows.shape
    units = weights.shape[1] // 2

    def body(x_ref, w_ref, p_ref, h_ref):
        both = contract(x_ref[...], w_ref[...], 1, 0)
        p_ref[...] = both
        gate = both[:, :block]
        h_ref[...] = (gate / (1.0 + jnp.exp(-gate)) * both[:, block:]).astype(BF)

    return pl.pallas_call(
        body,
        grid=(units // block,),
        in_specs=[
            pl.BlockSpec((group, width), lambda j: (0, 0)),
            pl.BlockSpec((width, 2 * block), lambda j: (0, j)),
        ],
        out_specs=[
            pl.BlockSpec((group, 2 * block), lambda j: (0, j)),
            pl.BlockSpec((group, block), lambda j: (0, j)),
        ],
        out_shape=[
            jax.ShapeDtypeStruct((group, 2 * units), F32),
            jax.ShapeDtypeStruct((group, units), BF),
        ],
        cost_estimate=cost(4 * group * width * units, rows, weights),
        compiler_params=pltpu.CompilerParams(vmem_limit_bytes=48 << 20),
        name="pair_forward",
    )(rows, weights)


def pick_halves(array, axis):
    dp = lax.axis_size("dp")
    first = lax.axis_index("dp") % 2 == 0
    share = array.shape[axis] // dp
    chunks = [lax.slice_in_dim(array, i * share, (i + 1) * share, axis=axis) for i in range(dp)]
    even = jnp.concatenate(chunks[0::2], axis=axis)
    odd = jnp.concatenate(chunks[1::2], axis=axis)
    return jnp.where(first, odd, even), jnp.where(first, even, odd)


def swap_cores(value):
    return lax.ppermute(value, "dp", [(i, i ^ 1) for i in range(lax.axis_size("dp"))])


def pair_sum(product, sides):
    got = swap_cores(product(sides[0]).astype(BF))
    return (product(sides[1]) + got.astype(F32)).astype(BF)


def interleave(left, right, block):
    count = left.shape[1] // block
    parts = []
    for i in range(count):
        parts += [left[:, i * block : (i + 1) * block], right[:, i * block : (i + 1) * block]]
    return jnp.concatenate(parts, axis=1)


def scatter_pairs(value, axis):
    size = lax.axis_size("dp")
    groups = [list(range(core, size, 2)) for core in (0, 1)]
    return lax.psum_scatter(
        value, "dp", scatter_dimension=axis, axis_index_groups=groups, tiled=True
    )


def spread_over_dp(chunks):
    size = chunks.shape[0]
    me = lax.axis_index("dp")
    total = lax.dynamic_index_in_dim(chunks, me, 0, keepdims=False)
    for shift in range(1, size):
        sent = lax.dynamic_index_in_dim(chunks, me ^ shift, 0, keepdims=False)
        total = total + lax.ppermute(sent, "dp", [(i, i ^ shift) for i in range(size)])
    return total


def layer(
    inputs, teacher, segment, position, wq, wk, wv, wo, wg, wu, wd, q_gain, k_gain, attn_gain, ffn_gain
):
    dp = lax.axis_size("dp")
    tensor = lax.axis_size("tensor")
    ring = Square(tensor) if tensor == 4 else Plain(tensor)
    rows, width = inputs.shape
    share, local_width = wq.shape
    units = wg.shape[1]
    heads_here = local_width // HD
    group = segment.shape[0]
    assert group == LEN and rows * tensor == group

    pieces = local_width // share
    wo_side = jnp.concatenate([wo[i * share : (i + 1) * share] for i in range(pieces)], axis=1)
    attn_shard = jnp.concatenate([wq, wk, wv, wo_side], axis=1)
    attn_all = lax.all_gather(attn_shard, "dp", axis=0, tiled=True)
    pair_all = lax.all_gather(interleave(wg, wu, BLOCK), "dp", axis=0, tiled=True)
    full_down = lax.all_gather(wd, "dp", axis=1, tiled=True)

    counted = jnp.sum((segment != 0).astype(F32))
    small = jnp.concatenate(
        [
            jnp.stack([q_gain, k_gain, attn_gain, ffn_gain]).astype(F32),
            jnp.broadcast_to(counted, (4, share)),
        ]
    )
    small_all = lax.all_gather(small, "dp", axis=1)
    gains = small_all[:4].reshape(4, width)
    valid_total = jnp.sum(small_all[4, :, 0])
    offset = ring.me * local_width
    gain_qk = lax.dynamic_slice(gains, (0, offset), (2, local_width))
    gain_attn = gains[2]
    gain_ffn = gains[3]

    segment_rel = jnp.take(segment.reshape(tensor, rows), ring.order, axis=0).reshape(group)
    position_rel = jnp.take(position.reshape(tensor, rows), ring.order, axis=0).reshape(group)
    place = (ring.order[:, None] * rows + jnp.arange(rows)[None, :]).reshape(group)
    allowed = (segment_rel[:, None] == segment_rel[None, :]) & (place[:, None] >= place[None, :])
    bias = jnp.where(
        (segment_rel[:, None] == segment_rel[None, :]) & (place[:, None] <= place[None, :]), 0.0, NEGATIVE
    )
    cosines, sines = tables(position_rel)
    flat_cosines = cosines[:, 0]
    flat_sines = jnp.concatenate([-sines[:, 0, : HD // 2], sines[:, 0, HD // 2 :]], axis=1)

    whole_inputs = ring.gather(inputs)
    qkv = attn_all[:, : 3 * local_width]
    full_out = (
        attn_all[:, 3 * local_width :]
        .reshape(dp, share, pieces, share)
        .transpose(2, 1, 0, 3)
        .reshape(local_width, width)
    )
    raw = times(whole_inputs, qkv)
    raw_q = raw[:, :local_width]
    raw_k = raw[:, local_width : 2 * local_width]
    value = raw[:, 2 * local_width :].astype(BF)
    squares = ring.total_by_token(jnp.stack([jnp.sum(raw_q * raw_q, axis=1), jnp.sum(raw_k * raw_k, axis=1)]))
    scales = lax.rsqrt(squares / width + EPS)
    scale_q = scales[0][:, None]
    scale_k = scales[1][:, None]
    normed_q = raw_q * scale_q
    normed_k = raw_k * scale_k
    query = rotate(
        (normed_q * gain_qk[0]).reshape(group, heads_here, HD), cosines, sines
    ).astype(BF)
    key = rotate((normed_k * gain_qk[1]).reshape(group, heads_here, HD), cosines, sines).astype(BF)
    mixed, logsum = attend_forward(query, key, value.reshape(group, heads_here, HD), allowed)
    query = query.reshape(group, local_width)
    key = key.reshape(group, local_width)
    attn_rows = mixed.reshape(group, local_width)
    branch_attn = ring.scatter(times(attn_rows, full_out))
    scale_attn = lax.rsqrt(jnp.mean(branch_attn * branch_attn, axis=1, keepdims=True) + EPS)
    normed_attn = branch_attn * scale_attn
    resid = inputs.astype(F32) + normed_attn * gain_attn
    whole_h = ring.gather(resid.astype(BF))

    pair, hidden = pair_forward(whole_h, pair_all)
    my_segment = lax.dynamic_slice_in_dim(segment, ring.me * rows, rows)
    valid = (my_segment != 0).astype(F32)
    valid = jnp.stack([valid, valid * (2.0 * (rows * dp * tensor) / valid_total)], axis=1)
    rest = (resid, teacher, valid, gain_ffn)
    if tensor == 4:
        half = rows // 2
        own, arrived_a, arrived_b = ring.scatter_product(hidden, full_down)
        *kept, upper, sums_a = loss_and_back(own, arrived_a, *rest, 0, half)
        output, grad_output, lower, sums_b = loss_and_back(own, arrived_b, *rest, half, rows, kept)
        sums = sums_a + sums_b
    else:
        own = ring.scatter_product(hidden, full_down)
        output, grad_output, grad_branch_ffn, sums = loss_and_back(own, (), *rest, 0, rows)
    grad_gain_ffn = sums[0]
    loss_part = jnp.sum(sums[1])
    if tensor == 4:
        got_rows = ring.gather_halves(upper, lower)
        cut = 3 * rows
        near_halves = pick_halves(jnp.concatenate(got_rows[:6], axis=0), 1)
        far_halves = pick_halves(jnp.concatenate(got_rows[6:], axis=0), 1)
        near = lax.optimization_barrier(
            tuple(inner_rows(hidden[:cut], half) for half in near_halves)
        )
        theirs = (near[0] + inner_rows(hidden[cut:], far_halves[0])).astype(BF)
        got = swap_cores(theirs)
        grad_down = near[1] + inner_rows(hidden[cut:], far_halves[1])
        grad_down = (grad_down + got.astype(F32)).astype(BF)
        piece = jnp.concatenate(got_rows, axis=0)
    else:
        piece = ring.gather(grad_branch_ffn)
        grad_down = pair_sum(lambda side: inner_rows(hidden, side), pick_halves(piece, 1))
    sum_down = scatter_pairs(grad_down, 1)
    piece, grad_down = lax.optimization_barrier((piece, grad_down))
    grad_pair = pair_backward(piece, full_down, pair)
    mine = pick_halves(whole_h, 1)
    theirs = inner_rows(mine[0], grad_pair).astype(BF)
    grad_pair, theirs = lax.optimization_barrier((grad_pair, theirs))
    got = swap_cores(theirs)
    back_h = times_transposed(grad_pair, pair_all)
    back_h, grad_pair = lax.optimization_barrier((back_h, grad_pair))
    back_h = ring.scatter(back_h)
    pair_grads = (inner_rows(mine[1], grad_pair) + got.astype(F32)).astype(BF)
    sum_pair = scatter_pairs(pair_grads, 0)
    back_h, pair_grads = lax.optimization_barrier((back_h, pair_grads))
    grad_resid = grad_output + back_h
    grad_gain_attn = jnp.sum(grad_resid * normed_attn, axis=0)
    grad_normed = grad_resid * gain_attn
    grad_branch_attn = (
        scale_attn
        * (grad_normed - normed_attn * jnp.mean(grad_normed * normed_attn, axis=1, keepdims=True))
    ).astype(BF)
    piece = ring.gather(grad_branch_attn)
    grad_mixed = times_transposed(piece, full_out).astype(BF)
    out_grads = pair_sum(lambda side: inner_rows(attn_rows, side), pick_halves(piece, 1))
    out_grads = (
        out_grads.reshape(pieces, share, dp // 2, share)
        .transpose(2, 1, 0, 3)
        .reshape(dp // 2 * share, pieces * share)
    )
    grad_normed_q, grad_normed_k, grad_value = attend_backward(
        query, key, value, grad_mixed, logsum, bias, flat_cosines, flat_sines
    )
    grad_hat_q = grad_normed_q * gain_qk[0]
    grad_hat_k = grad_normed_k * gain_qk[1]
    inner = ring.total_by_token(
        jnp.stack([jnp.sum(grad_hat_q * normed_q, axis=1), jnp.sum(grad_hat_k * normed_k, axis=1)])
    )
    grad_raw_q = (scale_q * (grad_hat_q - normed_q * (inner[0] / width)[:, None])).astype(BF)
    grad_raw_k = (scale_k * (grad_hat_k - normed_k * (inner[1] / width)[:, None])).astype(BF)
    grad_raw = jnp.concatenate([grad_raw_q, grad_raw_k, grad_value], axis=1)
    qkv_grads = pair_sum(lambda side: inner_rows(side, grad_raw), pick_halves(whole_inputs, 1))
    attn_grads = jnp.concatenate([qkv_grads, out_grads], axis=1)
    sum_attn = scatter_pairs(attn_grads, 0)
    grad_raw, attn_grads = lax.optimization_barrier((grad_raw, attn_grads))
    back_x = times_transposed(grad_raw, qkv)
    grad_input = grad_resid + ring.scatter(back_x)

    placed_q = lax.dynamic_update_slice_in_dim(
        jnp.zeros((width,), F32), jnp.sum(grad_normed_q * normed_q, axis=0), offset, 0
    )
    placed_k = lax.dynamic_update_slice_in_dim(
        jnp.zeros((width,), F32), jnp.sum(grad_normed_k * normed_k, axis=0), offset, 0
    )
    late = jnp.stack(
        [placed_q, placed_k, grad_gain_attn, grad_gain_ffn, jnp.broadcast_to(loss_part, (width,))]
    )
    late = jnp.concatenate([late, jnp.zeros((3, width), F32)])
    late = ring.total(late)
    late = spread_over_dp(late.reshape(8, dp, share).transpose(1, 0, 2))
    loss = late[4, 0] / (valid_total * width)

    sum_attn = sum_attn.astype(F32)
    sum_out = sum_attn[:, 3 * local_width :].reshape(share, pieces, share)
    sum_out = sum_out.transpose(1, 0, 2).reshape(local_width, share)
    sum_pair = sum_pair.astype(F32).reshape(share, units // BLOCK, 2, BLOCK)
    return (
        output,
        loss,
        grad_input,
        sum_attn[:, :local_width],
        sum_attn[:, local_width : 2 * local_width],
        sum_attn[:, 2 * local_width : 3 * local_width],
        sum_out,
        sum_pair[:, :, 0].reshape(share, units),
        sum_pair[:, :, 1].reshape(share, units),
        sum_down.astype(F32),
        late[0],
        late[1],
        late[2],
        late[3],
    )


def solution(mesh):
    cols = P("dp", "tensor")
    side = P("tensor", "dp")
    both = P(("dp", "tensor"), None)
    one = P("dp")
    return jax.shard_map(
        layer,
        mesh=mesh,
        in_specs=(both, both, one, one, cols, cols, cols, side, cols, cols, side, one, one, one, one),
        out_specs=(both, P(), both, cols, cols, cols, side, cols, cols, side, one, one, one, one),
        check_vma=False,
    )
```

```python
import jax
import jax.numpy as jnp
from jax import lax
from jax.experimental import pallas as pl
from jax.experimental.pallas import tpu as pltpu
from jax.sharding import PartitionSpec as P


HD = 128
LEN = 1024
EPS = 1e-06
THETA = 500000.0
NEGATIVE = -1e30
BLOCK = 256
BF = jnp.bfloat16
F32 = jnp.float32


def tables(position):
    freq = 1.0 / THETA ** (jnp.arange(0, HD, 2).astype(F32) / HD)
    angle = position.astype(F32)[:, None] * freq[None, :]
    angle = jnp.concatenate([angle, angle], axis=1)[:, None, :]
    return (jnp.cos(angle), jnp.sin(angle))


def rotate(values, cosines, sines):
    half = values.shape[-1] // 2
    turned = jnp.concatenate([-values[..., half:], values[..., :half]], axis=-1)
    return values * cosines + turned * sines


def inner_rows(left, right):
    return lax.dot_general(left, right, (((0,), (0,)), ((), ())), preferred_element_type=F32)


def times(left, right):
    return jnp.dot(left, right, preferred_element_type=F32)


def times_transposed(left, right):
    return lax.dot_general(left, right, (((1,), (1,)), ((), ())), preferred_element_type=F32)


def hop(value, way, size=4):
    return lax.ppermute(value, "tensor", [(i, i ^ way) for i in range(size)])


class Square:
    def __init__(self, size):
        self.size = size
        self.me = lax.axis_index("tensor")
        self.order = self.me ^ jnp.arange(size)

    def gather_halves(self, upper, lower):
        across_a = hop(upper, 1)
        along_a = hop(upper, 2)
        across_b = hop(lower, 1)
        along_b = hop(lower, 2)
        first = hop(across_a, 2)
        second = hop(along_b, 1)
        return upper, lower, across_a, across_b, along_a, along_b, first, second

    def gather(self, own):
        half = own.shape[0] // 2
        across = hop(own, 1)
        along = hop(own, 2)
        first = hop(across[:half], 2)
        second = hop(along[half:], 1)
        return jnp.concatenate([own, across, along, first, second], axis=0)

    def scatter_product(self, left, right):
        rows = left.shape[0] // 4
        half = rows // 2
        far = times(left[3 * rows :], right).astype(BF)
        first = hop(far[:half], 1)
        second = hop(far[half:], 2)
        near = lax.optimization_barrier(times(left[rows : 3 * rows], right))
        across_a = hop(near[:half].astype(BF), 1)
        along_a = hop((near[rows : rows + half] + first.astype(F32)).astype(BF), 2)
        across_b = hop((near[half:rows] + second.astype(F32)).astype(BF), 1)
        along_b = hop(near[rows + half :].astype(BF), 2)
        own = times(left[:rows], right)
        return own, (across_a, along_a), (across_b, along_b)

    def scatter(self, parts):
        rows = parts.shape[0] // 4
        half = rows // 2
        own, across, along, far = (parts[i * rows : (i + 1) * rows] for i in range(4))
        far = far.astype(BF)
        first = hop(far[:half], 1).astype(F32)
        second = hop(far[half:], 2).astype(F32)
        along = jnp.concatenate([along[:half] + first, along[half:]], axis=0).astype(BF)
        across = jnp.concatenate([across[:half], across[half:] + second], axis=0).astype(BF)
        across = hop(across, 1)
        along = hop(along, 2)
        return own + across.astype(F32) + along.astype(F32)

    def total(self, value):
        return (value + hop(value, 1)) + (hop(value, 2) + hop(value, 3))

    def total_by_token(self, value):
        blocks = value.reshape(value.shape[0], 4, -1)
        result = blocks
        for way in (1, 2, 3):
            got = hop(blocks, way)
            result = result + jnp.stack([got[:, r ^ way] for r in range(4)], axis=1)
        return result.reshape(value.shape)


class Plain:
    def __init__(self, size):
        self.size = size
        self.me = lax.axis_index("tensor")
        self.order = jnp.arange(size)

    def gather(self, own):
        return lax.all_gather(own, "tensor", axis=0, tiled=True)

    def scatter_product(self, left, right):
        return self.scatter(times(left, right))

    def scatter(self, parts):
        return lax.psum_scatter(
            parts.astype(BF), "tensor", scatter_dimension=0, tiled=True
        ).astype(F32)

    def total(self, value):
        return lax.psum(value, "tensor")

    def total_by_token(self, value):
        return lax.psum(value, "tensor")


def attend_forward(query, key, value, allowed):
    scores = jnp.einsum("qhd,khd->hqk", query, key, preferred_element_type=F32) * HD ** (-0.5)
    scores = jnp.where(allowed[None], scores, NEGATIVE)
    highest = jnp.max(scores, axis=-1, keepdims=True)
    raised = jnp.exp(scores - highest)
    total = jnp.sum(raised, axis=-1, keepdims=True)
    prob = (raised / total).astype(BF)
    mixed = jnp.einsum("hqk,khd->qhd", prob, value, preferred_element_type=F32)
    return (mixed.astype(BF), (highest + jnp.log(total))[..., 0])


def contract(left, right, left_axis, right_axis):
    return lax.dot_general(
        left, right, (((left_axis,), (right_axis,)), ((), ())), preferred_element_type=F32
    )


def cost(flops, *arrays):
    moved = sum(a.size * jnp.dtype(a.dtype).itemsize for a in arrays)
    return pl.CostEstimate(flops=flops, bytes_accessed=moved, transcendentals=0)


def turn_back(grad, cosine, sine):
    return grad * cosine + pltpu.roll(grad * sine, HD // 2, 1)


def join_attention(wq, wk, wv, wo):
    share, width = wq.shape
    side = wo.shape[1]

    def body(q_ref, k_ref, v_ref, o_ref, out_ref):
        for i, ref in enumerate((q_ref, k_ref, v_ref)):
            out_ref[:, i * width : (i + 1) * width] = ref[...]
        for i in range(wo.shape[0] // share):
            start = 3 * width + i * side
            out_ref[:, start : start + side] = o_ref[i * share : (i + 1) * share, :]

    return pl.pallas_call(
        body,
        out_shape=jax.ShapeDtypeStruct((share, 3 * width + wo.size // share), BF),
        cost_estimate=cost(0, wq, wk, wv, wo, wq, wk, wv, wo),
        name="join_attention",
    )(wq, wk, wv, wo)


def attend_backward(query, key, value, grad_mixed, logsum, bias, cosine, sine, block=512):
    group, width = query.shape
    heads = width // HD
    factor = HD ** (-0.5)
    steps = group // block

    def body(q_ref, k_ref, v_ref, g_ref, l_ref, b_ref, c_ref, s_ref, cq_ref, sq_ref, dq_ref, dk_ref, dv_ref, ak, av):
        head = pl.program_id(0)
        step = pl.program_id(1)

        @pl.when(step == 0)
        def _():
            ak[...] = jnp.zeros_like(ak)
            av[...] = jnp.zeros_like(av)

        q = q_ref[...]
        k = k_ref[...]
        g = g_ref[...]
        scores = contract(k, q, 1, 1) * factor + b_ref[...]
        prob = jnp.exp(scores - l_ref[pl.ds(head, 1), :])
        grad_prob = contract(v_ref[...], g, 1, 1)
        delta = jnp.sum(prob * grad_prob, axis=0, keepdims=True)
        grad_scores = (prob * (grad_prob - delta)).astype(BF)
        av[...] += contract(prob.astype(BF), g, 1, 0)
        ak[...] += contract(grad_scores, q, 1, 0)
        dq_ref[...] = turn_back(contract(grad_scores, k, 0, 0) * factor, cq_ref[...], sq_ref[...])

        @pl.when(step == steps - 1)
        def _():
            dk_ref[...] = turn_back(ak[...] * factor, c_ref[...], s_ref[...])
            dv_ref[...] = av[...].astype(BF)

    part = pl.BlockSpec((block, HD), lambda h, i: (i, h))
    whole = pl.BlockSpec((group, HD), lambda h, i: (0, h))
    table = pl.BlockSpec((group, HD), lambda h, i: (0, 0))
    table_part = pl.BlockSpec((block, HD), lambda h, i: (i, 0))
    return pl.pallas_call(
        body,
        grid=(heads, steps),
        in_specs=[
            part, whole, whole, part,
            pl.BlockSpec((heads, block), lambda h, i: (0, i)),
            pl.BlockSpec((group, block), lambda h, i: (0, i)),
            table, table, table_part, table_part,
        ],
        out_specs=[part, whole, whole],
        out_shape=[
            jax.ShapeDtypeStruct((group, width), F32),
            jax.ShapeDtypeStruct((group, width), F32),
            jax.ShapeDtypeStruct((group, width), BF),
        ],
        scratch_shapes=[pltpu.VMEM((group, HD), F32), pltpu.VMEM((group, HD), F32)],
        cost_estimate=cost(10 * group * group * width, bias, query, key, value, grad_mixed),
        name="attend_backward",
    )(query, key, value, grad_mixed, logsum, bias, cosine, sine, cosine, sine)


def pair_backward(piece, down, pair, block=BLOCK):
    group, width = piece.shape
    units = down.shape[0]

    def body(g_ref, w_ref, p_ref, o_ref):
        grad = contract(g_ref[...], w_ref[...], 1, 1)
        gate = p_ref[:, :block]
        up = p_ref[:, block:]
        sigma = 1.0 / (1.0 + jnp.exp(-gate))
        o_ref[:, :block] = (grad * up * sigma * (1.0 + gate * (1.0 - sigma))).astype(BF)
        o_ref[:, block:] = (grad * (gate * sigma)).astype(BF)

    return pl.pallas_call(
        body,
        grid=(units // block,),
        in_specs=[
            pl.BlockSpec((group, width), lambda j: (0, 0)),
            pl.BlockSpec((block, width), lambda j: (j, 0)),
            pl.BlockSpec((group, 2 * block), lambda j: (0, j)),
        ],
        out_specs=pl.BlockSpec((group, 2 * block), lambda j: (0, j)),
        out_shape=jax.ShapeDtypeStruct((group, 2 * units), BF),
        cost_estimate=cost(2 * group * width * units, piece, down, pair),
        compiler_params=pltpu.CompilerParams(vmem_limit_bytes=48 << 20),
        name="pair_backward",
    )(piece, down, pair)


def loss_and_back(own, arrived, resid, teacher, valid, gain, first, last, kept=None, block=64):
    rows, width = resid.shape
    count = len(arrived)
    held = () if kept is None else tuple(kept)

    def body(*refs):
        own_ref, x_ref, t_ref, v_ref, w_ref = refs[:5]
        o_ref, g_ref, b_ref, sum_ref = refs[5 + count + len(held) :]
        branch = own_ref[...]
        for ref in refs[5 : 5 + count]:
            branch = branch + ref[...].astype(F32)
        scale = lax.rsqrt(jnp.mean(branch * branch, axis=1, keepdims=True) + EPS)
        normed = branch * scale
        out = x_ref[...] + normed * w_ref[...]
        o_ref[...] = out.astype(BF)
        error = out - t_ref[...].astype(F32)
        grad = error * v_ref[:, 1:2]
        g_ref[...] = grad
        back = grad * w_ref[...]
        inner = jnp.mean(back * normed, axis=1, keepdims=True)
        b_ref[...] = (scale * (back - normed * inner)).astype(BF)

        @pl.when(pl.program_id(0) == 0)
        def _():
            sum_ref[...] = jnp.zeros_like(sum_ref)

        sum_ref[0:1, :] += jnp.sum(grad * normed, axis=0, keepdims=True)
        sum_ref[1:2, :] += jnp.sum(error * error * v_ref[:, 0:1], axis=0, keepdims=True)

    skip = first // block
    row = pl.BlockSpec((block, width), lambda i: (i + skip, 0))
    part = pl.BlockSpec((block, width), lambda i: (i, 0))
    arrays = (own, resid, teacher)
    return pl.pallas_call(
        body,
        grid=((last - first) // block,),
        in_specs=[row] * 3
        + [
            pl.BlockSpec((block, 2), lambda i: (i + skip, 0)),
            pl.BlockSpec((1, width), lambda i: (0, 0)),
        ]
        + [part] * count
        + [pl.BlockSpec(memory_space=pl.ANY)] * len(held),
        out_specs=[row, row, part, pl.BlockSpec((8, width), lambda i: (0, 0))],
        out_shape=[
            jax.ShapeDtypeStruct((rows, width), BF),
            jax.ShapeDtypeStruct((rows, width), F32),
            jax.ShapeDtypeStruct((last - first, width), BF),
            jax.ShapeDtypeStruct((8, width), F32),
        ],
        input_output_aliases={5 + count + i: i for i in range(len(held))},
        cost_estimate=cost(30 * (last - first) * width, *arrived, *arrived),
        name="loss_and_back",
    )(*arrays, valid, gain.reshape(1, width), *arrived, *held)


def pair_forward(rows, weights, block=BLOCK):
    group, width = rows.shape
    units = weights.shape[1] // 2

    def body(x_ref, w_ref, p_ref, h_ref):
        both = contract(x_ref[...], w_ref[...], 1, 0)
        p_ref[...] = both
        gate = both[:, :block]
        h_ref[...] = (gate / (1.0 + jnp.exp(-gate)) * both[:, block:]).astype(BF)

    return pl.pallas_call(
        body,
        grid=(units // block,),
        in_specs=[
            pl.BlockSpec((group, width), lambda j: (0, 0)),
            pl.BlockSpec((width, 2 * block), lambda j: (0, j)),
        ],
        out_specs=[
            pl.BlockSpec((group, 2 * block), lambda j: (0, j)),
            pl.BlockSpec((group, block), lambda j: (0, j)),
        ],
        out_shape=[
            jax.ShapeDtypeStruct((group, 2 * units), F32),
            jax.ShapeDtypeStruct((group, units), BF),
        ],
        cost_estimate=cost(4 * group * width * units, rows, weights),
        compiler_params=pltpu.CompilerParams(vmem_limit_bytes=48 << 20),
        name="pair_forward",
    )(rows, weights)


def pick_halves(array, axis):
    dp = lax.axis_size("dp")
    first = lax.axis_index("dp") % 2 == 0
    share = array.shape[axis] // dp
    chunks = [lax.slice_in_dim(array, i * share, (i + 1) * share, axis=axis) for i in range(dp)]
    even = jnp.concatenate(chunks[0::2], axis=axis)
    odd = jnp.concatenate(chunks[1::2], axis=axis)
    return jnp.where(first, odd, even), jnp.where(first, even, odd)


def swap_cores(value):
    return lax.ppermute(value, "dp", [(i, i ^ 1) for i in range(lax.axis_size("dp"))])


def pair_sum(product, sides):
    got = swap_cores(product(sides[0]).astype(BF))
    return (product(sides[1]) + got.astype(F32)).astype(BF)


def interleave(left, right, block):
    count = left.shape[1] // block
    parts = []
    for i in range(count):
        parts += [left[:, i * block : (i + 1) * block], right[:, i * block : (i + 1) * block]]
    return jnp.concatenate(parts, axis=1)


def scatter_pairs(value, axis):
    size = lax.axis_size("dp")
    groups = [list(range(core, size, 2)) for core in (0, 1)]
    return lax.psum_scatter(
        value, "dp", scatter_dimension=axis, axis_index_groups=groups, tiled=True
    )


def spread_over_dp(chunks):
    size = chunks.shape[0]
    me = lax.axis_index("dp")
    total = lax.dynamic_index_in_dim(chunks, me, 0, keepdims=False)
    for shift in range(1, size):
        sent = lax.dynamic_index_in_dim(chunks, me ^ shift, 0, keepdims=False)
        total = total + lax.ppermute(sent, "dp", [(i, i ^ shift) for i in range(size)])
    return total


def layer(
    inputs, teacher, segment, position, wq, wk, wv, wo, wg, wu, wd, q_gain, k_gain, attn_gain, ffn_gain
):
    dp = lax.axis_size("dp")
    tensor = lax.axis_size("tensor")
    ring = Square(tensor) if tensor == 4 else Plain(tensor)
    rows, width = inputs.shape
    share, local_width = wq.shape
    units = wg.shape[1]
    heads_here = local_width // HD
    group = segment.shape[0]
    assert group == LEN and rows * tensor == group

    pieces = local_width // share
    attn_shard = join_attention(wq, wk, wv, wo)
    attn_all = lax.all_gather(attn_shard, "dp", axis=0, tiled=True)
    pair_all = lax.all_gather(interleave(wg, wu, BLOCK), "dp", axis=0, tiled=True)
    full_down = lax.all_gather(wd, "dp", axis=1, tiled=True)

    counted = jnp.sum((segment != 0).astype(F32))
    small = jnp.concatenate(
        [
            jnp.stack([q_gain, k_gain, attn_gain, ffn_gain]).astype(F32),
            jnp.broadcast_to(counted, (4, share)),
        ]
    )
    small_all = lax.all_gather(small, "dp", axis=1)
    gains = small_all[:4].reshape(4, width)
    valid_total = jnp.sum(small_all[4, :, 0])
    offset = ring.me * local_width
    gain_qk = lax.dynamic_slice(gains, (0, offset), (2, local_width))
    gain_attn = gains[2]
    gain_ffn = gains[3]

    segment_rel = jnp.take(segment.reshape(tensor, rows), ring.order, axis=0).reshape(group)
    position_rel = jnp.take(position.reshape(tensor, rows), ring.order, axis=0).reshape(group)
    place = (ring.order[:, None] * rows + jnp.arange(rows)[None, :]).reshape(group)
    allowed = (segment_rel[:, None] == segment_rel[None, :]) & (place[:, None] >= place[None, :])
    bias = jnp.where(
        (segment_rel[:, None] == segment_rel[None, :]) & (place[:, None] <= place[None, :]), 0.0, NEGATIVE
    )
    cosines, sines = tables(position_rel)
    flat_cosines = cosines[:, 0]
    flat_sines = jnp.concatenate([-sines[:, 0, : HD // 2], sines[:, 0, HD // 2 :]], axis=1)

    whole_inputs = ring.gather(inputs)
    qkv = attn_all[:, : 3 * local_width]
    full_out = (
        attn_all[:, 3 * local_width :]
        .reshape(dp, share, pieces, share)
        .transpose(2, 1, 0, 3)
        .reshape(local_width, width)
    )
    raw = times(whole_inputs, qkv)
    raw_q = raw[:, :local_width]
    raw_k = raw[:, local_width : 2 * local_width]
    value = raw[:, 2 * local_width :].astype(BF)
    squares = ring.total_by_token(jnp.stack([jnp.sum(raw_q * raw_q, axis=1), jnp.sum(raw_k * raw_k, axis=1)]))
    scales = lax.rsqrt(squares / width + EPS)
    scale_q = scales[0][:, None]
    scale_k = scales[1][:, None]
    normed_q = raw_q * scale_q
    normed_k = raw_k * scale_k
    query = rotate(
        (normed_q * gain_qk[0]).reshape(group, heads_here, HD), cosines, sines
    ).astype(BF)
    key = rotate((normed_k * gain_qk[1]).reshape(group, heads_here, HD), cosines, sines).astype(BF)
    mixed, logsum = attend_forward(query, key, value.reshape(group, heads_here, HD), allowed)
    query = query.reshape(group, local_width)
    key = key.reshape(group, local_width)
    attn_rows = mixed.reshape(group, local_width)
    branch_attn = ring.scatter(times(attn_rows, full_out))
    scale_attn = lax.rsqrt(jnp.mean(branch_attn * branch_attn, axis=1, keepdims=True) + EPS)
    normed_attn = branch_attn * scale_attn
    resid = inputs.astype(F32) + normed_attn * gain_attn
    whole_h = ring.gather(resid.astype(BF))

    pair, hidden = pair_forward(whole_h, pair_all)
    my_segment = lax.dynamic_slice_in_dim(segment, ring.me * rows, rows)
    valid = (my_segment != 0).astype(F32)
    valid = jnp.stack([valid, valid * (2.0 * (rows * dp * tensor) / valid_total)], axis=1)
    rest = (resid, teacher, valid, gain_ffn)
    if tensor == 4:
        half = rows // 2
        own, arrived_a, arrived_b = ring.scatter_product(hidden, full_down)
        *kept, upper, sums_a = loss_and_back(own, arrived_a, *rest, 0, half)
        output, grad_output, lower, sums_b = loss_and_back(own, arrived_b, *rest, half, rows, kept)
        sums = sums_a + sums_b
    else:
        own = ring.scatter_product(hidden, full_down)
        output, grad_output, grad_branch_ffn, sums = loss_and_back(own, (), *rest, 0, rows)
    grad_gain_ffn = sums[0]
    loss_part = jnp.sum(sums[1])
    if tensor == 4:
        got_rows = ring.gather_halves(upper, lower)
        cut = 3 * rows
        near_halves = pick_halves(jnp.concatenate(got_rows[:6], axis=0), 1)
        far_halves = pick_halves(jnp.concatenate(got_rows[6:], axis=0), 1)
        near = lax.optimization_barrier(
            tuple(inner_rows(hidden[:cut], half) for half in near_halves)
        )
        theirs = (near[0] + inner_rows(hidden[cut:], far_halves[0])).astype(BF)
        got = swap_cores(theirs)
        grad_down = near[1] + inner_rows(hidden[cut:], far_halves[1])
        grad_down = (grad_down + got.astype(F32)).astype(BF)
        piece = jnp.concatenate(got_rows, axis=0)
    else:
        piece = ring.gather(grad_branch_ffn)
        grad_down = pair_sum(lambda side: inner_rows(hidden, side), pick_halves(piece, 1))
    sum_down = scatter_pairs(grad_down, 1)
    piece, grad_down = lax.optimization_barrier((piece, grad_down))
    grad_pair = pair_backward(piece, full_down, pair)
    mine = pick_halves(whole_h, 1)
    theirs = inner_rows(mine[0], grad_pair).astype(BF)
    grad_pair, theirs = lax.optimization_barrier((grad_pair, theirs))
    got = swap_cores(theirs)
    back_h = times_transposed(grad_pair, pair_all)
    back_h, grad_pair = lax.optimization_barrier((back_h, grad_pair))
    back_h = ring.scatter(back_h)
    pair_grads = (inner_rows(mine[1], grad_pair) + got.astype(F32)).astype(BF)
    sum_pair = scatter_pairs(pair_grads, 0)
    back_h, pair_grads = lax.optimization_barrier((back_h, pair_grads))
    grad_resid = grad_output + back_h
    grad_gain_attn = jnp.sum(grad_resid * normed_attn, axis=0)
    grad_normed = grad_resid * gain_attn
    grad_branch_attn = (
        scale_attn
        * (grad_normed - normed_attn * jnp.mean(grad_normed * normed_attn, axis=1, keepdims=True))
    ).astype(BF)
    piece = ring.gather(grad_branch_attn)
    grad_mixed = times_transposed(piece, full_out).astype(BF)
    out_grads = pair_sum(lambda side: inner_rows(attn_rows, side), pick_halves(piece, 1))
    out_grads = (
        out_grads.reshape(pieces, share, dp // 2, share)
        .transpose(2, 1, 0, 3)
        .reshape(dp // 2 * share, pieces * share)
    )
    grad_normed_q, grad_normed_k, grad_value = attend_backward(
        query, key, value, grad_mixed, logsum, bias, flat_cosines, flat_sines
    )
    grad_hat_q = grad_normed_q * gain_qk[0]
    grad_hat_k = grad_normed_k * gain_qk[1]
    inner = ring.total_by_token(
        jnp.stack([jnp.sum(grad_hat_q * normed_q, axis=1), jnp.sum(grad_hat_k * normed_k, axis=1)])
    )
    grad_raw_q = (scale_q * (grad_hat_q - normed_q * (inner[0] / width)[:, None])).astype(BF)
    grad_raw_k = (scale_k * (grad_hat_k - normed_k * (inner[1] / width)[:, None])).astype(BF)
    grad_raw = jnp.concatenate([grad_raw_q, grad_raw_k, grad_value], axis=1)
    qkv_grads = pair_sum(lambda side: inner_rows(side, grad_raw), pick_halves(whole_inputs, 1))
    attn_grads = jnp.concatenate([qkv_grads, out_grads], axis=1)
    sum_attn = scatter_pairs(attn_grads, 0)
    grad_raw, attn_grads = lax.optimization_barrier((grad_raw, attn_grads))
    back_x = times_transposed(grad_raw, qkv)
    grad_input = grad_resid + ring.scatter(back_x)

    placed_q = lax.dynamic_update_slice_in_dim(
        jnp.zeros((width,), F32), jnp.sum(grad_normed_q * normed_q, axis=0), offset, 0
    )
    placed_k = lax.dynamic_update_slice_in_dim(
        jnp.zeros((width,), F32), jnp.sum(grad_normed_k * normed_k, axis=0), offset, 0
    )
    late = jnp.stack(
        [placed_q, placed_k, grad_gain_attn, grad_gain_ffn, jnp.broadcast_to(loss_part, (width,))]
    )
    late = jnp.concatenate([late, jnp.zeros((3, width), F32)])
    late = ring.total(late)
    late = spread_over_dp(late.reshape(8, dp, share).transpose(1, 0, 2))
    loss = late[4, 0] / (valid_total * width)

    sum_attn = sum_attn.astype(F32)
    sum_out = sum_attn[:, 3 * local_width :].reshape(share, pieces, share)
    sum_out = sum_out.transpose(1, 0, 2).reshape(local_width, share)
    sum_pair = sum_pair.astype(F32).reshape(share, units // BLOCK, 2, BLOCK)
    return (
        output,
        loss,
        grad_input,
        sum_attn[:, :local_width],
        sum_attn[:, local_width : 2 * local_width],
        sum_attn[:, 2 * local_width : 3 * local_width],
        sum_out,
        sum_pair[:, :, 0].reshape(share, units),
        sum_pair[:, :, 1].reshape(share, units),
        sum_down.astype(F32),
        late[0],
        late[1],
        late[2],
        late[3],
    )


def solution(mesh):
    cols = P("dp", "tensor")
    side = P("tensor", "dp")
    both = P(("dp", "tensor"), None)
    one = P("dp")
    return jax.shard_map(
        layer,
        mesh=mesh,
        in_specs=(both, both, one, one, cols, cols, cols, side, cols, cols, side, one, one, one, one),
        out_specs=(both, P(), both, cols, cols, cols, side, cols, cols, side, one, one, one, one),
        check_vma=False,
    )
```
